32 devices in a mesh: group: 2 (over x), wide: 2 (over core), tensor: 8 (over z, y).
Axes of the slice: x: 2, y: 2, z: 4, core: 2. Of those that a mesh axis runs over, the one named last changes fastest.
Arguments:
- tokens: bfloat16 [512, 8192], P(('group', 'wide'), 'tensor'), parts along dimension 0, may hold values from -6 to 6
- gain: float32 [16384], P('group'), parts along dimension 0, may hold values from 0.5 to 2
- gate_weight: bfloat16 [16384, 16384], P(('group', 'wide', 'tensor')), parts along dimension 0, may hold values from -0.09375 to 0.09375
- up_weight: bfloat16 [16384, 16384], P(('group', 'wide', 'tensor')), parts along dimension 0, may hold values from -0.09375 to 0.09375
- gate_mask: int32 [256, 256], P('group'), parts along dimension 0, may hold values from 0 to 1, as said below
- up_mask: int32 [256, 256], P('group'), parts along dimension 0, may hold values from 0 to 1, as said below
Outputs:
- hidden: bfloat16 [512, 16384], P(('group', 'wide'), 'tensor'), parts along dimension 0
The draws below stay inside these ranges and needn't reach their ends.
There are 2 independent parts, one for each index of `group`. The reference program is written for one: setup_inputs(seed, part) draws one part's arguments, and reference() takes and returns one part's arrays. A program takes and returns all parts, laid end to end along the dimension named above; each array names one. Nothing has to cross between parts.
Inputs may be any that keep to these rules, and one draw needn't show every extreme that they name: `gate_mask`: A 1 keeps a block, a 0 prunes it; the share of kept blocks differs between groups of consecutive hidden-unit blocks. `up_mask`: as for gate_mask.
All inputs are finite; a program needn't handle non-finite values.
Results may differ from the reference program's by a relative error of at most 0.0058.
Values may be sent and summed in bfloat16 or wider, within the bound.
A program may use at most 256 MiB of HBM per device.

```python
import math
import jax
import jax.numpy as jnp
from jax import lax

D = 8192
FF = 16384
BS = 64
TOKENS = 256
N_TENSOR = 8


def mask_draw(key, rows, cols, groups):
    first = jax.random.fold_in(key, 11)
    second = jax.random.fold_in(key, 23)
    levels = jax.random.randint(first, (groups,), 1, 4)
    limits = jnp.repeat(levels, cols // groups)[None, :]
    draws = jax.random.randint(second, (rows, cols), 0, 4)
    return (draws < limits).astype(jnp.int32)


def draw_gate_mask(key, part):
    return mask_draw(jax.random.fold_in(key, 1), D // BS, FF // BS, N_TENSOR)


def draw_up_mask(key, part):
    return mask_draw(jax.random.fold_in(key, 2), D // BS, FF // BS, N_TENSOR)


def steps_of(own_key, dims, shards, low, top_value):
    level = 1.0
    for axis_at, blocks in shards:
        heights = jax.random.uniform(jax.random.fold_in(jax.random.fold_in(own_key, 6), axis_at), (blocks,), jnp.float32, low / len(shards), top_value / len(shards))
        level = level * jnp.repeat(jnp.exp(heights), dims[axis_at] // blocks).reshape((-1,) + (1,) * (len(dims) - 1 - axis_at))
    return level


def normal_values(rng, dims, scale, limit, pieces=(), held_as=jnp.bfloat16):
    entries = scale * jax.random.normal(rng, dims, jnp.float32)
    if pieces:
        entries = entries * steps_of(rng, dims, pieces, -0.22, 0.18)
    return jnp.clip(entries, -limit, limit).astype(held_as)


def setup_inputs(seed: int = 0, part: int = 0) -> dict:
    seeds = jax.random.split(jax.random.key(seed), 7)
    own_keys = jax.random.split(jax.random.fold_in(seeds[6], part), 7)
    return {
        "tokens": normal_values(own_keys[0], (TOKENS, D), 1.0, 6.0, ((0, 2), (1, 8))),
        "gain": jnp.clip(jnp.exp(jax.random.uniform(own_keys[1], (D,), jnp.float32, math.log(0.5), math.log(2.0))), 0.5, 2.0),
        "gate_weight": normal_values(own_keys[2], (D, FF), (D // 2) ** -0.5, 0.09375, ((0, 16),)),
        "up_weight": normal_values(own_keys[3], (D, FF), (D // 2) ** -0.5, 0.09375, ((0, 16),)),
        "gate_mask": draw_gate_mask(jax.random.fold_in(jax.random.fold_in(seeds[6], part), 71), part),
        "up_mask": draw_up_mask(jax.random.fold_in(jax.random.fold_in(seeds[6], part), 71), part),
    }


def expand(mask, weight):
    rows, cols = mask.shape
    blocks = weight.reshape(rows, BS, cols, BS) * mask.astype(jnp.bfloat16)[:, None, :, None]
    return blocks.reshape(weight.shape)

def reference(tokens, gain, gate_weight, up_weight, gate_mask, up_mask):
    values = tokens.astype(jnp.float32)
    scale = lax.rsqrt(lax.optimization_barrier(jnp.mean(values * values, axis=-1, keepdims=True)) + 1e-05)
    normed = (values * scale * gain).astype(jnp.bfloat16)
    gate = jnp.dot(normed, expand(gate_mask, gate_weight), preferred_element_type=jnp.float32)
    up = jnp.dot(normed, expand(up_mask, up_weight), preferred_element_type=jnp.float32)
    return (jax.nn.silu(gate) * up).astype(jnp.bfloat16)
```

```python
import functools

import jax
import jax.numpy as jnp
from jax import lax
from jax.experimental import pallas as pl
from jax.experimental.pallas import tpu as pltpu
from jax.sharding import PartitionSpec as P

BS = 64
SUB = 512
LAG = 3
MID_LAG = 10
W_SLOTS = 4
X_SLOTS = 4
EPS = 1e-05
MESH = pl.DeviceIdType.MESH


def kernel(
    nt, ny, sub, tok_ref, gain_ref, gw_hbm, uw_hbm, gm_ref, um_ref, out_ref,
    stats, stat_out, xbuf, xs, mine, wbuf, own, xsend, xrecv, ysend, yrecv, zsend, zrecv, orecv,
    stat_ssem, stat_rsem, tok_ssem, tok_rsem, wsem, x_ssem, x_rsem, y_ssem, y_rsem, z_ssem, z_rsem, o_ssem, o_rsem,
):
    nz = nt // ny
    w = lax.axis_index("wide")
    t = lax.axis_index("tensor")
    z, y = lax.div(t, ny), lax.rem(t, ny)
    me = w * nt + t
    peers = 2 * nt
    rows, feats = tok_ref.shape
    depth, ff = gw_hbm.shape
    width = ff // nt
    per = width // sub
    pairs = nz * per
    units = 2 * pairs
    blocks = depth // BS

    def at(dev):
        return {"wide": lax.div(dev, nt), "tensor": lax.rem(dev, nt)}

    early = max(1, per // 2)
    low = z < nz - 1 - z
    corner = (z == 0) | (z == nz - 1)
    side = jnp.where(low, z, nz - 1 - z)

    def defers(plane, dest, q):
        to = jnp.where(plane == 0, 1, jnp.where(plane == nz - 1, nz - 2, -1))
        if nz >= 4:
            to = jnp.where(plane == 1, 0, jnp.where(plane == nz - 2, nz - 1, to))
        limit = jnp.where((plane == 0) | (plane == nz - 1), early, per)
        return (to >= 0) & (to < nz) & (dest == to) & (q < limit)

    def mid_order(i):
        k = lax.div(i, per)
        right, left = nz - 1 - z, z
        both = jnp.minimum(right, left)
        paired = k < 2 * both
        idx = jnp.where(paired, lax.div(k, 2), k - both)
        is_right = jnp.where(paired, (lax.rem(k, 2) == 0) == (right > left), right > left)
        dest = jnp.where(is_right, nz - 1 - idx, idx)
        dest = jnp.where(k == nz - 1, z, dest)
        return dest, lax.rem(i, per)

    def corner_order(i):
        ahead = jnp.minimum(lax.div(i + 1, 2), early)
        first = (lax.rem(i, 2) == 1) & (i < 2 * early)
        j = i - ahead
        far, near = (nz - 2) * per, (nz - 1) * per - early
        dest = jnp.where(j < far, nz - 1 - lax.div(j, per), jnp.where(j < near, 1, 0))
        q = jnp.where(j < far, lax.rem(j, per), jnp.where(j < near, j - far + early, j - near))
        dest = jnp.where(first, 1, dest)
        q = jnp.where(first, lax.div(i, 2), q)
        return jnp.where(low, dest, nz - 1 - dest), q

    def task(i):
        if nz == 1:
            return jnp.int32(0), i
        dest_m, q_m = mid_order(i)
        dest_c, q_c = corner_order(i)
        return jnp.where(corner, dest_c, dest_m), jnp.where(corner, q_c, q_m)

    def column(unit):
        pair, kind = lax.div(unit, 2), lax.rem(unit, 2)
        y_to = jnp.where(kind == 0, ny - 1 - y, y)
        dest, q = task(pair)
        owner = dest * ny + y_to
        return pl.multiple_of(owner * width + q * sub, 128)

    def weight_copies(unit):
        slot = lax.rem(unit, W_SLOTS)
        cols = pl.ds(column(unit), sub)
        return (
            pltpu.make_async_copy(gw_hbm.at[:, cols], wbuf.at[slot, 0], wsem.at[slot, 0]),
            pltpu.make_async_copy(uw_hbm.at[:, cols], wbuf.at[slot, 1], wsem.at[slot, 1]),
        )

    def fetch(unit):
        for copy in weight_copies(unit):
            copy.start()

    for unit in range(min(W_SLOTS, units)):
        fetch(jnp.int32(unit))

    barrier = pltpu.get_barrier_semaphore()

    @pl.loop(1, peers)
    def _(d):
        pl.semaphore_signal(
            barrier, inc=1, device_id=at(lax.rem(me + d, peers)), device_id_type=MESH
        )

    total = jnp.zeros((rows, 128), jnp.float32)
    for f in range(0, feats, 128):
        v = tok_ref[:, f:f + 128].astype(jnp.float32)
        total = total + v * v
    line = jnp.sum(total.T, axis=0, keepdims=True)
    stat_out[...] = jnp.broadcast_to(line, (8, rows))
    stats[me] = jnp.broadcast_to(line, (8, rows))

    pl.semaphore_wait(barrier, peers - 1)

    def token_copy(h):
        dev = 2 * t + h
        return dev, pltpu.make_async_remote_copy(
            src_ref=tok_ref.at[:, h * depth:(h + 1) * depth],
            dst_ref=xbuf.at[w],
            send_sem=tok_ssem.at[h],
            recv_sem=tok_rsem.at[w],
            device_id=at(dev),
            device_id_type=MESH,
        )

    def stat_copy(d, src):
        return pltpu.make_async_remote_copy(
            src_ref=stat_out,
            dst_ref=stats.at[src],
            send_sem=stat_ssem.at[d],
            recv_sem=stat_rsem.at[src],
            device_id=at(lax.rem(me + d, peers)),
            device_id_type=MESH,
        )

    @pl.loop(1, peers)
    def _(d):
        stat_copy(d, me).start()

    for h in range(2):
        dev, copy = token_copy(h)

        @pl.when(dev != me)
        def _():
            copy.start()

        @pl.when(dev == me)
        def _():
            xbuf[w] = tok_ref[:, h * depth:(h + 1) * depth]

    mrows = gm_ref.shape[0]
    pick = (
        lax.broadcasted_iota(jnp.int32, (8, mrows), 1)
        == lax.broadcasted_iota(jnp.int32, (8, mrows), 0) + me * blocks
    ).astype(jnp.float32).astype(jnp.bfloat16)
    for a, m_ref in enumerate((gm_ref, um_ref)):
        kept = m_ref[...].astype(jnp.float32).astype(jnp.bfloat16)
        mine[a * 8:(a + 1) * 8, :] = jnp.dot(pick, kept, preferred_element_type=jnp.float32)
    mcols = gm_ref.shape[1]

    @pl.loop(1, peers)
    def _(d):
        stat_copy(d, lax.rem(me + d, peers)).wait_recv()

    for v in range(2):
        @pl.when(v * nt + lax.div(me, 2) != me)
        def _():
            pltpu.make_async_remote_copy(
                src_ref=tok_ref.at[:, 0:depth], dst_ref=xbuf.at[v],
                send_sem=tok_ssem.at[0], recv_sem=tok_rsem.at[v],
                device_id=at(lax.rem(me + 1, peers)), device_id_type=MESH,
            ).wait_recv()

    gain = gain_ref[:, pl.ds(pl.multiple_of(me * depth, 128), depth)]
    for half in range(2):
        v = w if half == 0 else 1 - w
        ssq = jnp.sum(stats[pl.ds(v * nt, nt)], axis=0)[0:1, :]
        scale = lax.rsqrt(ssq / (feats * nt) + EPS)
        scale = jnp.broadcast_to(scale, (rows, rows)).T[:, 0:1]
        xs[half * rows:(half + 1) * rows, :] = (
            xbuf[v].astype(jnp.float32) * scale * gain
        ).astype(jnp.bfloat16)

    def x_copy(unit):
        slot = lax.rem(unit, X_SLOTS)
        return pltpu.make_async_remote_copy(
            src_ref=xsend.at[slot], dst_ref=xrecv.at[unit],
            send_sem=x_ssem.at[slot], recv_sem=x_rsem.at[unit],
            device_id={"wide": 1 - w}, device_id_type=MESH,
        )

    def y_copy(pair):
        return pltpu.make_async_remote_copy(
            src_ref=ysend.at[pair], dst_ref=yrecv.at[pair],
            send_sem=y_ssem.at[pair], recv_sem=y_rsem.at[pair],
            device_id={"tensor": z * ny + (ny - 1 - y)}, device_id_type=MESH,
        )

    def z_copy(pair, side, piece, z_to):
        return pltpu.make_async_remote_copy(
            src_ref=zsend.at[pair], dst_ref=zrecv.at[side, piece],
            send_sem=z_ssem.at[pair], recv_sem=z_rsem.at[side, piece],
            device_id={"tensor": z_to * ny + y}, device_id_type=MESH,
        )

    def other_copy(pair, q, side_to, z_to):
        return pltpu.make_async_remote_copy(
            src_ref=ysend.at[pair], dst_ref=orecv.at[side_to, q],
            send_sem=o_ssem.at[q], recv_sem=o_rsem.at[side_to, q],
            device_id={"tensor": z_to * ny + y}, device_id_type=MESH,
        )

    def compute(unit):
        slot = lax.rem(unit, W_SLOTS)
        xslot = lax.rem(unit, X_SLOTS)
        first = lax.broadcasted_iota(jnp.int32, (mcols, sub), 0) * BS - column(unit)
        col = lax.broadcasted_iota(jnp.int32, (mcols, sub), 1)
        spread = ((col >= first) & (col < first + BS)).astype(jnp.float32).astype(jnp.bfloat16)
        mexp = jnp.dot(mine[...].astype(jnp.bfloat16), spread, preferred_element_type=jnp.float32)
        for copy in weight_copies(unit):
            copy.wait()

        @pl.when(unit >= X_SLOTS)
        def _():
            x_copy(unit - X_SLOTS).wait_send()

        for a in range(2):
            kept = []
            for r in range(blocks):
                keep = jnp.broadcast_to(mexp[a * 8 + r:a * 8 + r + 1, :], (BS, sub)).astype(jnp.bfloat16)
                kept.append(wbuf[slot, a, r * BS:(r + 1) * BS, :] * keep)
            part = jnp.dot(
                xs[...], jnp.concatenate(kept, axis=0), preferred_element_type=jnp.float32
            )
            own[xslot, :, a * sub:(a + 1) * sub] = part[:rows]
            xsend[xslot, :, a * sub:(a + 1) * sub] = part[rows:]
        x_copy(unit).start()

        @pl.when(unit + W_SLOTS < units)
        def _():
            fetch(unit + W_SLOTS)

    def finish(unit, kind):
        pair = lax.div(unit, 2)
        x_copy(unit).wait_recv()
        both = own[lax.rem(unit, X_SLOTS)] + xrecv[unit]
        xrecv[unit] = both
        if kind == 0:
            dest, q = task(pair)
            for s, away in ((0, -1), (1, 1)):
                @pl.when((dest == z) & (z + away >= 0) & (z + away < nz) & defers(z + away, z, q))
                def _():
                    other_copy(pair, q, s, lax.rem(z + 1, nz)).wait_recv()
                    xrecv[unit] = xrecv[unit] + orecv[s, q].astype(jnp.float32)

            ysend[pair] = xrecv[unit].astype(jnp.bfloat16)
            late = defers(z, dest, q)

            @pl.when(jnp.logical_not(late))
            def _():
                y_copy(pair).start()

            @pl.when(late & (dest > z))
            def _():
                other_copy(pair, q, 0, z + 1).start()

            @pl.when(late & (dest < z))
            def _():
                other_copy(pair, q, 1, z - 1).start()

    def settle(pair):
        unit = 2 * pair + 1
        dest, q = task(pair)
        piece = dest * per + q

        @pl.when(jnp.logical_not(defers(z, dest, q)))
        def _():
            y_copy(pair).wait_recv()
            xrecv[unit] = xrecv[unit] + yrecv[pair].astype(jnp.float32)

        @pl.when((dest >= z) & (z > 0))
        def _():
            z_copy(pair, 0, piece, z - 1).wait_recv()
            xrecv[unit] = xrecv[unit] + zrecv[0, piece].astype(jnp.float32)

        @pl.when((dest <= z) & (z < nz - 1))
        def _():
            z_copy(pair, 1, piece, z + 1).wait_recv()
            xrecv[unit] = xrecv[unit] + zrecv[1, piece].astype(jnp.float32)

        @pl.when(dest != z)
        def _():
            zsend[pair] = xrecv[unit].astype(jnp.bfloat16)

        @pl.when(dest > z)
        def _():
            z_copy(pair, 0, piece, z + 1).start()

        @pl.when(dest < z)
        def _():
            z_copy(pair, 1, piece, z - 1).start()

        @pl.when(dest == z)
        def _():
            g = xrecv[unit, :, 0:sub]
            u = xrecv[unit, :, sub:2 * sub]
            at_col = pl.multiple_of(q * sub, 128)
            out_ref[:, pl.ds(at_col, sub)] = (g / (1.0 + jnp.exp(-g)) * u).astype(out_ref.dtype)

    lag = jnp.where(corner, LAG, MID_LAG)

    @pl.loop(0, pairs + max(LAG, MID_LAG))
    def _(i):
        @pl.when(i < pairs)
        def _():
            compute(2 * i)

        @pl.when((i >= 1) & (i <= pairs))
        def _():
            finish(2 * i - 1, 1)

        @pl.when(i < pairs)
        def _():
            finish(2 * i, 0)
            compute(2 * i + 1)

        @pl.when((i >= lag) & (i < pairs + lag))
        def _():
            settle(i - lag)

    for unit in range(max(0, units - X_SLOTS), units):
        x_copy(jnp.int32(unit)).wait_send()

    @pl.loop(0, pairs)
    def _(pair):
        dest, q = task(pair)
        late = defers(z, dest, q)

        @pl.when(jnp.logical_not(late))
        def _():
            y_copy(pair).wait_send()

        @pl.when(late)
        def _():
            other_copy(pair, q, 0, lax.rem(z + 1, nz)).wait_send()

        @pl.when(dest != z)
        def _():
            z_copy(pair, 0, pair, lax.rem(z + 1, nz)).wait_send()

    @pl.loop(1, peers)
    def _(d):
        stat_copy(d, me).wait_send()

    for h in range(2):
        dev, copy = token_copy(h)

        @pl.when(dev != me)
        def _():
            copy.wait_send()


def local(tokens, gain, gate_weight, up_weight, gate_mask, up_mask):
    nt = lax.axis_size("tensor")
    ny = 2
    rows, feats = tokens.shape
    depth, ff = gate_weight.shape
    width = ff // nt
    sub = min(SUB, width)
    per = width // sub
    pairs = (nt // ny) * per
    peers = 2 * nt
    dma = pltpu.SemaphoreType.DMA
    vmem = pl.BlockSpec(memory_space=pltpu.VMEM)
    hbm = pl.BlockSpec(memory_space=pl.ANY)
    tile = (rows, 2 * sub)
    return pl.pallas_call(
        functools.partial(kernel, nt, ny, sub),
        out_shape=jax.ShapeDtypeStruct((rows, width), jnp.bfloat16),
        in_specs=[vmem, vmem, hbm, hbm, vmem, vmem],
        out_specs=vmem,
        scratch_shapes=[
            pltpu.VMEM((peers, 8, rows), jnp.float32),
            pltpu.VMEM((8, rows), jnp.float32),
            pltpu.VMEM((2, rows, depth), jnp.bfloat16),
            pltpu.VMEM((2 * rows, depth), jnp.bfloat16),
            pltpu.VMEM((16, gate_mask.shape[1]), jnp.float32),
            pltpu.VMEM((W_SLOTS, 2, depth, sub), jnp.bfloat16),
            pltpu.VMEM((X_SLOTS,) + tile, jnp.float32),
            pltpu.VMEM((X_SLOTS,) + tile, jnp.float32),
            pltpu.VMEM((2 * pairs,) + tile, jnp.float32),
            pltpu.VMEM((pairs,) + tile, jnp.bfloat16),
            pltpu.VMEM((pairs,) + tile, jnp.bfloat16),
            pltpu.VMEM((pairs,) + tile, jnp.bfloat16),
            pltpu.VMEM((2, pairs) + tile, jnp.bfloat16),
            pltpu.VMEM((2, per) + tile, jnp.bfloat16),
            dma((peers,)), dma((peers,)), dma((2,)), dma((2,)), dma((W_SLOTS, 2)),
            dma((X_SLOTS,)), dma((2 * pairs,)), dma((pairs,)), dma((pairs,)),
            dma((pairs,)), dma((2, pairs)), dma((per,)), dma((2, per)),
        ],
        compiler_params=pltpu.CompilerParams(
            collective_id=0, has_side_effects=True, vmem_limit_bytes=60 * 1024 * 1024
        ),
    )(tokens, gain.reshape(1, -1), gate_weight, up_weight, gate_mask, up_mask)


def solution(mesh):
    in_specs = (
        P(("group", "wide"), "tensor"),
        P("group"),
        P(("group", "wide", "tensor"), None),
        P(("group", "wide", "tensor"), None),
        P("group", None),
        P("group", None),
    )
    out_specs = P(("group", "wide"), "tensor")
    return jax.shard_map(local, mesh=mesh, in_specs=in_specs, out_specs=out_specs, check_vma=False)
```

```python
import functools

import jax
import jax.numpy as jnp
from jax import lax
from jax.experimental import pallas as pl
from jax.experimental.pallas import tpu as pltpu
from jax.sharding import PartitionSpec as P

BS = 64
SUB = 512
LAG = 2
MID_LAG = 10
PRE = 2
W_SLOTS = 4
X_SLOTS = 4
EPS = 1e-05
MESH = pl.DeviceIdType.MESH


def kernel(
    nt, ny, sub, tok_hbm, gain_hbm, gw_hbm, uw_hbm, gm_hbm, um_hbm, out_ref,
    tok, gain_all, masks, stats, stat_out, xbuf, xs, mine, wbuf, own, xsend, xrecv, osum,
    ysend, yrecv, zsend, zrecv, orecv,
    in_sem, stat_ssem, stat_rsem, tok_ssem, tok_rsem, wsem, x_ssem, x_rsem, h_ssem, h_rsem,
    y_ssem, y_rsem, z_ssem, z_rsem, o_ssem, o_rsem,
):
    nz = nt // ny
    w = lax.axis_index("wide")
    t = lax.axis_index("tensor")
    z, y = lax.div(t, ny), lax.rem(t, ny)
    me = w * nt + t
    peers = 2 * nt
    rows, feats = tok.shape
    hrows = rows // 2
    depth, ff = gw_hbm.shape
    width = ff // nt
    per = width // sub
    pairs = nz * per
    units = 2 * pairs
    blocks = depth // BS

    def at(dev):
        return {"wide": lax.div(dev, nt), "tensor": lax.rem(dev, nt)}

    barrier = pltpu.get_barrier_semaphore()

    @pl.loop(1, peers)
    def _(d):
        pl.semaphore_signal(
            barrier, inc=1, device_id=at(lax.rem(me + d, peers)), device_id_type=MESH
        )

    loads = (
        pltpu.make_async_copy(tok_hbm, tok, in_sem.at[0]),
        pltpu.make_async_copy(gm_hbm, masks.at[0], in_sem.at[1]),
        pltpu.make_async_copy(um_hbm, masks.at[1], in_sem.at[2]),
        pltpu.make_async_copy(gain_hbm, gain_all, in_sem.at[3]),
    )
    for copy in loads:
        copy.start()

    early = max(1, per // 2)
    low = z < nz - 1 - z
    corner = (z == 0) | (z == nz - 1)

    def defers(plane, dest, q):
        to = jnp.where(plane == 1, 0, jnp.where(plane == nz - 2, nz - 1, -1))
        to = jnp.where(plane == 0, 1, jnp.where(plane == nz - 1, nz - 2, to))
        limit = jnp.where((plane == 0) | (plane == nz - 1), early, per)
        return (dest == to) & (q < limit)

    def mid_order(i):
        k = lax.div(i, per)
        right, left = nz - 1 - z, z
        both = jnp.minimum(right, left)
        paired = k < 2 * both
        idx = jnp.where(paired, lax.div(k, 2), k - both)
        is_right = jnp.where(paired, (lax.rem(k, 2) == 0) == (right > left), right > left)
        dest = jnp.where(is_right, nz - 1 - idx, idx)
        dest = jnp.where(k == nz - 1, z, dest)
        return dest, lax.rem(i, per)

    def corner_order(i):
        ahead = jnp.minimum(lax.div(i + 1, 2), early)
        first = (lax.rem(i, 2) == 1) & (i < 2 * early)
        j = i - ahead
        far, near = (nz - 2) * per, (nz - 1) * per - early
        dest = jnp.where(j < far, nz - 1 - lax.div(j, per), jnp.where(j < near, 1, 0))
        q = jnp.where(j < far, lax.rem(j, per), jnp.where(j < near, j - far + early, j - near))
        dest = jnp.where(first, 1, dest)
        q = jnp.where(first, lax.div(i, 2), q)
        return jnp.where(low, dest, nz - 1 - dest), q

    def task(i):
        dest_m, q_m = mid_order(i)
        dest_c, q_c = corner_order(i)
        return jnp.where(corner, dest_c, dest_m), jnp.where(corner, q_c, q_m)

    def split(unit):
        r = lax.rem(unit, 4)
        return 2 * lax.div(unit, 4) + lax.rem(r, 2), lax.div(r, 2)

    def column(unit):
        pair, kind = split(unit)
        y_to = jnp.where(kind == 0, ny - 1 - y, y)
        dest, q = task(pair)
        owner = dest * ny + y_to
        return pl.multiple_of(owner * width + q * sub, 128)

    def weight_copies(unit):
        slot = lax.rem(unit, W_SLOTS)
        cols = pl.ds(column(unit), sub)
        return (
            pltpu.make_async_copy(gw_hbm.at[:, cols], wbuf.at[slot, 0], wsem.at[slot]),
            pltpu.make_async_copy(uw_hbm.at[:, cols], wbuf.at[slot, 1], wsem.at[slot]),
        )

    def fetch(unit):
        for copy in weight_copies(unit):
            copy.start()

    def fetched(unit):
        slot = lax.rem(unit, W_SLOTS)
        pltpu.make_async_copy(wbuf.at[slot], wbuf.at[slot], wsem.at[slot]).wait()

    for unit in range(min(W_SLOTS, units)):
        fetch(jnp.int32(unit))

    loads[0].wait()
    total = jnp.zeros((rows, 128), jnp.float32)
    for f in range(0, feats, 128):
        v = tok[:, f:f + 128].astype(jnp.float32)
        total = total + v * v
    line = jnp.sum(total.T, axis=0, keepdims=True)
    stat_out[...] = line
    stats[me] = line

    pl.semaphore_wait(barrier, peers - 1)

    def token_copy(h, r):
        dev = 2 * t + h
        return dev, pltpu.make_async_remote_copy(
            src_ref=tok.at[r * hrows:(r + 1) * hrows, h * depth:(h + 1) * depth],
            dst_ref=xbuf.at[w, r * hrows:(r + 1) * hrows, :],
            send_sem=tok_ssem.at[h, r],
            recv_sem=tok_rsem.at[w, r],
            device_id=at(dev),
            device_id_type=MESH,
        )

    @pl.loop(1, peers)
    def _(d):
        pltpu.make_async_remote_copy(
            src_ref=stat_out, dst_ref=stats.at[me], send_sem=stat_ssem, recv_sem=stat_rsem,
            device_id=at(lax.rem(me + d, peers)), device_id_type=MESH,
        ).start()

    for r in range(2):
        for h in range(2):
            dev, copy = token_copy(h, r)

            @pl.when(dev != me)
            def _():
                copy.start()

            @pl.when(dev == me)
            def _():
                xbuf[w, r * hrows:(r + 1) * hrows, :] = tok[
                    r * hrows:(r + 1) * hrows, h * depth:(h + 1) * depth
                ]

    for copy in loads[1:]:
        copy.wait()
    mrows, mcols = masks.shape[1:]
    pick = (
        lax.broadcasted_iota(jnp.int32, (8, mrows), 1)
        == lax.broadcasted_iota(jnp.int32, (8, mrows), 0) + me * blocks
    ).astype(jnp.float32).astype(jnp.bfloat16)
    for a in range(2):
        kept = masks[a].astype(jnp.float32).astype(jnp.bfloat16)
        mine[a * 8:(a + 1) * 8, :] = jnp.dot(pick, kept, preferred_element_type=jnp.float32)

    gain = gain_all[:, pl.ds(pl.multiple_of(me * depth, 128), depth)]

    def normalise(r):
        for v in range(2):
            @pl.when(v * nt + lax.div(me, 2) != me)
            def _():
                pltpu.make_async_remote_copy(
                    src_ref=tok.at[0:hrows, 0:depth],
                    dst_ref=xbuf.at[v, r * hrows:(r + 1) * hrows, :],
                    send_sem=tok_ssem.at[0, 0], recv_sem=tok_rsem.at[v, r],
                    device_id=at(lax.rem(me + 1, peers)), device_id_type=MESH,
                ).wait_recv()

        for half in range(2):
            v = w if half == 0 else 1 - w
            ssq = jnp.sum(stats[pl.ds(v * nt, nt)], axis=0)
            scale = lax.rsqrt(ssq / (feats * nt) + EPS)
            scale = jnp.broadcast_to(scale, (rows, rows)).T[r * hrows:(r + 1) * hrows, 0:1]
            first = (2 * r + half) * hrows
            xs[first:first + hrows, :] = (
                xbuf[v, r * hrows:(r + 1) * hrows, :].astype(jnp.float32) * scale * gain
            ).astype(jnp.bfloat16)

    def half_copy(unit, r):
        slot = lax.rem(unit, X_SLOTS)
        part = pl.ds(r * hrows, hrows)
        return pltpu.make_async_remote_copy(
            src_ref=xsend.at[slot, part, :], dst_ref=xrecv.at[slot, part, :],
            send_sem=h_ssem.at[unit, r], recv_sem=h_rsem.at[unit, r],
            device_id={"wide": 1 - w}, device_id_type=MESH,
        )

    def x_copy(unit):
        slot = lax.rem(unit, X_SLOTS)
        return pltpu.make_async_remote_copy(
            src_ref=xsend.at[slot], dst_ref=xrecv.at[slot],
            send_sem=x_ssem.at[slot], recv_sem=x_rsem.at[slot],
            device_id={"wide": 1 - w}, device_id_type=MESH,
        )

    def y_copy(pair, part):
        return pltpu.make_async_remote_copy(
            src_ref=ysend.at[pair, part, :], dst_ref=yrecv.at[pair, part, :],
            send_sem=y_ssem, recv_sem=y_rsem.at[pair],
            device_id={"tensor": z * ny + (ny - 1 - y)}, device_id_type=MESH,
        )

    def z_copy(pair, place, z_to):
        return pltpu.make_async_remote_copy(
            src_ref=zsend.at[pair], dst_ref=zrecv.at[place],
            send_sem=z_ssem, recv_sem=z_rsem.at[place],
            device_id={"tensor": z_to * ny + y}, device_id_type=MESH,
        )

    def other_copy(pair, q, z_to, part):
        return pltpu.make_async_remote_copy(
            src_ref=ysend.at[pair, part, :], dst_ref=orecv.at[q, part, :],
            send_sem=o_ssem, recv_sem=o_rsem.at[q],
            device_id={"tensor": z_to * ny + y}, device_id_type=MESH,
        )

    def products(unit, x):
        slot = lax.rem(unit, W_SLOTS)
        first = lax.broadcasted_iota(jnp.int32, (mcols, sub), 0) * BS - column(unit)
        col = lax.broadcasted_iota(jnp.int32, (mcols, sub), 1)
        spread = ((col >= first) & (col < first + BS)).astype(jnp.float32).astype(jnp.bfloat16)
        mexp = jnp.dot(mine[...].astype(jnp.bfloat16), spread, preferred_element_type=jnp.float32)
        for a in range(2):
            kept = []
            for r in range(blocks):
                keep = jnp.broadcast_to(mexp[a * 8 + r:a * 8 + r + 1, :], (BS, sub)).astype(jnp.bfloat16)
                kept.append(wbuf[slot, a, r * BS:(r + 1) * BS, :] * keep)
            yield a, jnp.dot(x, jnp.concatenate(kept, axis=0), preferred_element_type=jnp.float32)

    def compute_half(unit, r):
        xslot = lax.rem(unit, X_SLOTS)
        for a, part in products(unit, xs[2 * r * hrows:2 * (r + 1) * hrows, :]):
            own[xslot, r * hrows:(r + 1) * hrows, a * sub:(a + 1) * sub] = part[:hrows]
            xsend[xslot, r * hrows:(r + 1) * hrows, a * sub:(a + 1) * sub] = part[hrows:]
        half_copy(unit, r).start()

    def compute(unit):
        xslot = lax.rem(unit, X_SLOTS)
        fetched(unit)

        @pl.when(unit >= X_SLOTS + PRE)
        def _():
            x_copy(unit - X_SLOTS).wait_send()

        for a, part in products(unit, xs[...]):
            for r in range(2):
                at_row = slice(r * hrows, (r + 1) * hrows)
                own[xslot, at_row, a * sub:(a + 1) * sub] = part[2 * r * hrows:(2 * r + 1) * hrows]
                xsend[xslot, at_row, a * sub:(a + 1) * sub] = part[(2 * r + 1) * hrows:(2 * r + 2) * hrows]
        x_copy(unit).start()

        @pl.when(unit + W_SLOTS < units)
        def _():
            fetch(unit + W_SLOTS)

    def send_other(pair, part):
        dest, q = task(pair)
        late = defers(z, dest, q)

        @pl.when(jnp.logical_not(late))
        def _():
            y_copy(pair, part).start()

        @pl.when(late)
        def _():
            other_copy(pair, q, dest, part).start()

    def finish_half(unit, r):
        slot = lax.rem(unit, X_SLOTS)
        half_copy(unit, r).wait_recv()
        part = slice(r * hrows, (r + 1) * hrows)
        ysend[unit, part, :] = (own[slot, part, :] + xrecv[slot, part, :]).astype(jnp.bfloat16)
        send_other(unit, pl.ds(r * hrows, hrows))

    def finish(unit):
        pair, kind = split(unit)
        dest, q = task(pair)
        slot = lax.rem(unit, X_SLOTS)
        x_copy(unit).wait_recv()

        @pl.when(kind == 1)
        def _():
            osum[pair] = own[slot] + xrecv[slot]

        joined = (dest == z) & (defers(z - 1, z, q) | defers(z + 1, z, q))

        @pl.when((kind == 0) & joined)
        def _():
            other_copy(pair, q, lax.rem(z + 1, nz), pl.ds(0, rows)).wait_recv()
            ysend[pair] = (own[slot] + xrecv[slot] + orecv[q].astype(jnp.float32)).astype(jnp.bfloat16)

        @pl.when((kind == 0) & jnp.logical_not(joined))
        def _():
            ysend[pair] = (own[slot] + xrecv[slot]).astype(jnp.bfloat16)

        @pl.when(kind == 0)
        def _():
            send_other(pair, pl.ds(0, rows))

    def settle(pair):
        dest, q = task(pair)
        piece = dest * per + q

        @pl.when(jnp.logical_not(defers(z, dest, q)))
        def _():
            y_copy(pair, pl.ds(0, rows)).wait_recv()
            osum[pair] = osum[pair] + yrecv[pair].astype(jnp.float32)

        below = (dest >= z) & (z > 0)
        above = (dest <= z) & (z < nz - 1)

        @pl.when(below)
        def _():
            z_copy(pair, piece, z - 1).wait_recv()
            osum[pair] = osum[pair] + zrecv[piece].astype(jnp.float32)

        @pl.when(above)
        def _():
            place = jnp.where(dest == z, pairs + q, piece)
            z_copy(pair, place, z + 1).wait_recv()
            osum[pair] = osum[pair] + zrecv[place].astype(jnp.float32)

        @pl.when(dest != z)
        def _():
            up = dest > z
            zsend[pair] = osum[pair].astype(jnp.bfloat16)
            place = jnp.where(dest == z - 1, pairs + q, piece)
            z_copy(pair, place, jnp.where(up, z + 1, z - 1)).start()

        @pl.when(dest == z)
        def _():
            g = osum[pair, :, 0:sub]
            u = osum[pair, :, sub:2 * sub]
            at_col = pl.multiple_of(q * sub, 128)
            out_ref[:, pl.ds(at_col, sub)] = (g / (1.0 + jnp.exp(-g)) * u).astype(out_ref.dtype)

    pltpu.make_async_copy(stats.at[1:], stats.at[1:], stat_rsem).wait()
    for r in range(2):
        normalise(r)

        @pl.loop(0, PRE)
        def _(unit):
            if r == 0:
                fetched(unit)
            compute_half(unit, r)

        @pl.loop(0, PRE)
        def _(unit):
            finish_half(unit, r)
            half_copy(unit, r).wait_send()
            if r == 1:
                @pl.when(unit + W_SLOTS < units)
                def _():
                    fetch(unit + W_SLOTS)

    lag = jnp.where(corner, LAG, MID_LAG)

    @pl.loop(PRE, units + 2 * max(LAG, MID_LAG) + 1)
    def _(u):
        @pl.when(u < units)
        def _():
            compute(u)

        @pl.when((u > PRE) & (u <= units))
        def _():
            finish(u - 1)

        j = lax.div(u - 1, 2) - lag

        @pl.when((lax.rem(u, 2) == 1) & (j >= 0) & (j < pairs))
        def _():
            settle(j)

    for unit in range(units - X_SLOTS, units):
        x_copy(jnp.int32(unit)).wait_send()

    def sent(buf, n, sem):
        pltpu.make_async_copy(buf.at[0:n], buf.at[0:n], sem).wait()

    near = (z == 1) | (z == nz - 2)
    for which, late in ((corner, early), (near, per), (jnp.logical_not(corner | near), 0)):
        @pl.when(which)
        def _():
            sent(ysend, pairs - late, y_ssem)
            if late:
                sent(ysend, late, o_ssem)

    sent(zsend, pairs - per, z_ssem)
    sent(stats, peers - 1, stat_ssem)
    for r in range(2):
        for h in range(2):
            dev, copy = token_copy(h, r)

            @pl.when(dev != me)
            def _():
                copy.wait_send()


def local(tokens, gain, gate_weight, up_weight, gate_mask, up_mask):
    nt = lax.axis_size("tensor")
    ny = 2
    rows, feats = tokens.shape
    depth, ff = gate_weight.shape
    width = ff // nt
    sub = min(SUB, width)
    per = width // sub
    pairs = (nt // ny) * per
    peers = 2 * nt
    dma = pltpu.SemaphoreType.DMA
    hbm = pl.BlockSpec(memory_space=pl.ANY)
    tile = (rows, 2 * sub)
    return pl.pallas_call(
        functools.partial(kernel, nt, ny, sub),
        out_shape=jax.ShapeDtypeStruct((rows, width), jnp.bfloat16),
        in_specs=[hbm] * 6,
        out_specs=pl.BlockSpec(memory_space=pltpu.VMEM),
        scratch_shapes=[
            pltpu.VMEM((rows, feats), jnp.bfloat16),
            pltpu.VMEM((1, gain.shape[0]), jnp.float32),
            pltpu.VMEM((2,) + gate_mask.shape, jnp.int32),
            pltpu.VMEM((peers, 1, rows), jnp.float32),
            pltpu.VMEM((1, rows), jnp.float32),
            pltpu.VMEM((2, rows, depth), jnp.bfloat16),
            pltpu.VMEM((2 * rows, depth), jnp.bfloat16),
            pltpu.VMEM((16, gate_mask.shape[1]), jnp.float32),
            pltpu.VMEM((W_SLOTS, 2, depth, sub), jnp.bfloat16),
            pltpu.VMEM((X_SLOTS,) + tile, jnp.float32),
            pltpu.VMEM((X_SLOTS,) + tile, jnp.float32),
            pltpu.VMEM((X_SLOTS,) + tile, jnp.float32),
            pltpu.VMEM((pairs,) + tile, jnp.float32),
            pltpu.VMEM((pairs,) + tile, jnp.bfloat16),
            pltpu.VMEM((pairs,) + tile, jnp.bfloat16),
            pltpu.VMEM((pairs,) + tile, jnp.bfloat16),
            pltpu.VMEM((pairs + per,) + tile, jnp.bfloat16),
            pltpu.VMEM((per,) + tile, jnp.bfloat16),
            dma((4,)), dma, dma, dma((2, 2)), dma((2, 2)), dma((W_SLOTS,)),
            dma((X_SLOTS,)), dma((X_SLOTS,)), dma((PRE, 2)), dma((PRE, 2)),
            dma, dma((pairs,)), dma, dma((pairs + per,)), dma, dma((per,)),
        ],
        compiler_params=pltpu.CompilerParams(
            collective_id=0, has_side_effects=True, vmem_limit_bytes=60 * 1024 * 1024
        ),
    )(tokens, gain.reshape(1, -1), gate_weight, up_weight, gate_mask, up_mask)


def solution(mesh):
    in_specs = (
        P(("group", "wide"), "tensor"),
        P("group"),
        P(("group", "wide", "tensor"), None),
        P(("group", "wide", "tensor"), None),
        P("group", None),
        P("group", None),
    )
    out_specs = P(("group", "wide"), "tensor")
    return jax.shard_map(local, mesh=mesh, in_specs=in_specs, out_specs=out_specs, check_vma=False)
```

```python
import functools

import jax
import jax.numpy as jnp
from jax import lax
from jax.experimental import pallas as pl
from jax.experimental.pallas import tpu as pltpu
from jax.sharding import PartitionSpec as P

BS = 64
SUB = 512
LAG = 0
MID_LAG = 9
PRE = 2
W_SLOTS = 4
X_SLOTS = 4
EPS = 1e-05
MESH = pl.DeviceIdType.MESH


def kernel(
    nt, ny, sub, tok_hbm, gain_hbm, gw_hbm, uw_hbm, gm_hbm, um_hbm, out_ref,
    tok, gain_all, masks, stats, stat_out, xbuf, xs, mine, wbuf, own, xsend, xrecv, osum,
    ysend, yrecv, zsend, zrecv, orecv,
    in_sem, stat_ssem, stat_rsem, tok_ssem, tok_rsem, wsem, x_ssem, x_rsem, h_ssem, h_rsem,
    y_ssem, y_rsem, z_ssem, z_rsem, o_ssem, o_rsem,
):
    nz = nt // ny
    w = lax.axis_index("wide")
    t = lax.axis_index("tensor")
    z, y = lax.div(t, ny), lax.rem(t, ny)
    me = w * nt + t
    peers = 2 * nt
    rows, feats = tok.shape
    hrows = rows // 2
    depth, ff = gw_hbm.shape
    width = ff // nt
    per = width // sub
    pairs = nz * per
    units = 2 * pairs
    blocks = depth // BS

    def at(dev):
        return {"wide": lax.div(dev, nt), "tensor": lax.rem(dev, nt)}

    barrier = pltpu.get_barrier_semaphore()

    @pl.loop(1, peers)
    def _(d):
        pl.semaphore_signal(
            barrier, inc=1, device_id=at(lax.rem(me + d, peers)), device_id_type=MESH
        )

    loads = (
        pltpu.make_async_copy(tok_hbm, tok, in_sem.at[0]),
        pltpu.make_async_copy(gm_hbm, masks.at[0], in_sem.at[1]),
        pltpu.make_async_copy(um_hbm, masks.at[1], in_sem.at[2]),
        pltpu.make_async_copy(gain_hbm, gain_all, in_sem.at[3]),
    )
    for copy in loads:
        copy.start()

    early = max(1, per // 2)
    low = z < nz - 1 - z
    corner = (z == 0) | (z == nz - 1)

    def defers(plane, dest, q):
        to = jnp.where(plane == 1, 0, jnp.where(plane == nz - 2, nz - 1, -1))
        to = jnp.where(plane == 0, 1, jnp.where(plane == nz - 1, nz - 2, to))
        limit = jnp.where((plane == 0) | (plane == nz - 1), early, per)
        return (dest == to) & (q < limit)

    def mid_order(i):
        k = lax.div(i, per)
        right, left = nz - 1 - z, z
        both = jnp.minimum(right, left)
        paired = k < 2 * both
        idx = jnp.where(paired, lax.div(k, 2), k - both)
        is_right = jnp.where(paired, (lax.rem(k, 2) == 0) == (right > left), right > left)
        dest = jnp.where(is_right, nz - 1 - idx, idx)
        dest = jnp.where(k == nz - 1, z, dest)
        return dest, lax.rem(i, per)

    def corner_order(i):
        ahead = jnp.minimum(lax.div(i + 1, 2), early)
        first = (lax.rem(i, 2) == 1) & (i < 2 * early)
        j = i - ahead
        far, near = (nz - 2) * per, (nz - 1) * per - early
        dest = jnp.where(j < far, nz - 1 - lax.div(j, per), jnp.where(j < near, 1, 0))
        q = jnp.where(j < far, lax.rem(j, per), jnp.where(j < near, j - far + early, j - near))
        dest = jnp.where(first, 1, dest)
        q = jnp.where(first, lax.div(i, 2), q)
        return jnp.where(low, dest, nz - 1 - dest), q

    def task(i):
        dest_m, q_m = mid_order(i)
        dest_c, q_c = corner_order(i)
        return jnp.where(corner, dest_c, dest_m), jnp.where(corner, q_c, q_m)

    def split(unit):
        m, odd = lax.div(unit, 2), lax.rem(unit, 2)
        ends = (unit < PRE) | (unit >= units - PRE)
        pair = jnp.where(unit < PRE, unit, jnp.where(ends, pairs - units + unit, m + 1 - 2 * odd))
        return pair, jnp.where(ends, (unit >= PRE).astype(jnp.int32), odd)

    def column(unit):
        pair, kind = split(unit)
        y_to = jnp.where(kind == 0, ny - 1 - y, y)
        dest, q = task(pair)
        owner = dest * ny + y_to
        return pl.multiple_of(owner * width + q * sub, 128)

    def weight_copies(unit):
        slot = lax.rem(unit, W_SLOTS)
        cols = pl.ds(column(unit), sub)
        return (
            pltpu.make_async_copy(gw_hbm.at[:, cols], wbuf.at[slot, 0], wsem.at[slot]),
            pltpu.make_async_copy(uw_hbm.at[:, cols], wbuf.at[slot, 1], wsem.at[slot]),
        )

    def fetch(unit):
        for copy in weight_copies(unit):
            copy.start()

    def fetched(unit):
        slot = lax.rem(unit, W_SLOTS)
        pltpu.make_async_copy(wbuf.at[slot], wbuf.at[slot], wsem.at[slot]).wait()

    for unit in range(min(W_SLOTS, units)):
        fetch(jnp.int32(unit))

    loads[0].wait()
    total = jnp.zeros((rows, 128), jnp.float32)
    for f in range(0, feats, 128):
        v = tok[:, f:f + 128].astype(jnp.float32)
        total = total + v * v
    line = jnp.sum(total.T, axis=0, keepdims=True)
    stat_out[...] = line
    stats[me] = line

    pl.semaphore_wait(barrier, peers - 1)

    def token_copy(h, r):
        dev = 2 * t + h
        return dev, pltpu.make_async_remote_copy(
            src_ref=tok.at[r * hrows:(r + 1) * hrows, h * depth:(h + 1) * depth],
            dst_ref=xbuf.at[w, r * hrows:(r + 1) * hrows, :],
            send_sem=tok_ssem.at[h, r],
            recv_sem=tok_rsem.at[w, r],
            device_id=at(dev),
            device_id_type=MESH,
        )

    @pl.loop(1, peers)
    def _(d):
        pltpu.make_async_remote_copy(
            src_ref=stat_out, dst_ref=stats.at[me], send_sem=stat_ssem, recv_sem=stat_rsem,
            device_id=at(lax.rem(me + d, peers)), device_id_type=MESH,
        ).start()

    for r in range(2):
        for h in range(2):
            dev, copy = token_copy(h, r)

            @pl.when(dev != me)
            def _():
                copy.start()

            @pl.when(dev == me)
            def _():
                xbuf[w, r * hrows:(r + 1) * hrows, :] = tok[
                    r * hrows:(r + 1) * hrows, h * depth:(h + 1) * depth
                ]

    for copy in loads[1:]:
        copy.wait()
    mrows, mcols = masks.shape[1:]
    pick = (
        lax.broadcasted_iota(jnp.int32, (8, mrows), 1)
        == lax.broadcasted_iota(jnp.int32, (8, mrows), 0) + me * blocks
    ).astype(jnp.float32).astype(jnp.bfloat16)
    for a in range(2):
        kept = masks[a].astype(jnp.float32).astype(jnp.bfloat16)
        mine[a * 8:(a + 1) * 8, :] = jnp.dot(pick, kept, preferred_element_type=jnp.float32)

    gain = gain_all[:, pl.ds(pl.multiple_of(me * depth, 128), depth)]

    def normalise(r):
        for v in range(2):
            @pl.when(v * nt + lax.div(me, 2) != me)
            def _():
                pltpu.make_async_remote_copy(
                    src_ref=tok.at[0:hrows, 0:depth],
                    dst_ref=xbuf.at[v, r * hrows:(r + 1) * hrows, :],
                    send_sem=tok_ssem.at[0, 0], recv_sem=tok_rsem.at[v, r],
                    device_id=at(lax.rem(me + 1, peers)), device_id_type=MESH,
                ).wait_recv()

        for half in range(2):
            v = w if half == 0 else 1 - w
            ssq = jnp.sum(stats[pl.ds(v * nt, nt)], axis=0)
            scale = lax.rsqrt(ssq / (feats * nt) + EPS)
            scale = jnp.broadcast_to(scale, (rows, rows)).T[r * hrows:(r + 1) * hrows, 0:1]
            first = (2 * r + half) * hrows
            xs[first:first + hrows, :] = (
                xbuf[v, r * hrows:(r + 1) * hrows, :].astype(jnp.float32) * scale * gain
            ).astype(jnp.bfloat16)

    def half_copy(unit, r):
        slot = lax.rem(unit, X_SLOTS)
        part = pl.ds(r * hrows, hrows)
        return pltpu.make_async_remote_copy(
            src_ref=xsend.at[slot, part, :], dst_ref=xrecv.at[slot, part, :],
            send_sem=h_ssem.at[unit, r], recv_sem=h_rsem.at[unit, r],
            device_id={"wide": 1 - w}, device_id_type=MESH,
        )

    def x_copy(unit):
        slot = lax.rem(unit, X_SLOTS)
        return pltpu.make_async_remote_copy(
            src_ref=xsend.at[slot], dst_ref=xrecv.at[slot],
            send_sem=x_ssem.at[slot], recv_sem=x_rsem.at[slot],
            device_id={"wide": 1 - w}, device_id_type=MESH,
        )

    def y_copy(pair, part):
        return pltpu.make_async_remote_copy(
            src_ref=ysend.at[pair, part, :], dst_ref=yrecv.at[pair, part, :],
            send_sem=y_ssem, recv_sem=y_rsem.at[pair],
            device_id={"tensor": z * ny + (ny - 1 - y)}, device_id_type=MESH,
        )

    def z_copy(pair, place, z_to):
        return pltpu.make_async_remote_copy(
            src_ref=zsend.at[pair], dst_ref=zrecv.at[place],
            send_sem=z_ssem, recv_sem=z_rsem.at[place],
            device_id={"tensor": z_to * ny + y}, device_id_type=MESH,
        )

    def other_copy(pair, q, z_to, part):
        return pltpu.make_async_remote_copy(
            src_ref=ysend.at[pair, part, :], dst_ref=orecv.at[q, part, :],
            send_sem=o_ssem, recv_sem=o_rsem.at[q],
            device_id={"tensor": z_to * ny + y}, device_id_type=MESH,
        )

    def products(unit, x):
        slot = lax.rem(unit, W_SLOTS)
        first = lax.broadcasted_iota(jnp.int32, (mcols, sub), 0) * BS - column(unit)
        col = lax.broadcasted_iota(jnp.int32, (mcols, sub), 1)
        spread = ((col >= first) & (col < first + BS)).astype(jnp.float32).astype(jnp.bfloat16)
        mexp = jnp.dot(mine[...].astype(jnp.bfloat16), spread, preferred_element_type=jnp.float32)
        for a in range(2):
            kept = []
            for r in range(blocks):
                keep = jnp.broadcast_to(mexp[a * 8 + r:a * 8 + r + 1, :], (BS, sub)).astype(jnp.bfloat16)
                kept.append(wbuf[slot, a, r * BS:(r + 1) * BS, :] * keep)
            yield a, jnp.dot(x, jnp.concatenate(kept, axis=0), preferred_element_type=jnp.float32)

    def compute_half(unit, r):
        xslot = lax.rem(unit, X_SLOTS)
        for a, part in products(unit, xs[2 * r * hrows:2 * (r + 1) * hrows, :]):
            own[xslot, r * hrows:(r + 1) * hrows, a * sub:(a + 1) * sub] = part[:hrows]
            xsend[xslot, r * hrows:(r + 1) * hrows, a * sub:(a + 1) * sub] = part[hrows:]
        half_copy(unit, r).start()

    def compute(unit):
        xslot = lax.rem(unit, X_SLOTS)
        fetched(unit)

        @pl.when(unit >= X_SLOTS + PRE)
        def _():
            x_copy(unit - X_SLOTS).wait_send()

        for a, part in products(unit, xs[...]):
            for r in range(2):
                at_row = slice(r * hrows, (r + 1) * hrows)
                own[xslot, at_row, a * sub:(a + 1) * sub] = part[2 * r * hrows:(2 * r + 1) * hrows]
                xsend[xslot, at_row, a * sub:(a + 1) * sub] = part[(2 * r + 1) * hrows:(2 * r + 2) * hrows]
        x_copy(unit).start()

        @pl.when(unit + W_SLOTS < units)
        def _():
            fetch(unit + W_SLOTS)

    def send_other(pair, part):
        dest, q = task(pair)
        late = defers(z, dest, q)

        @pl.when(jnp.logical_not(late))
        def _():
            y_copy(pair, part).start()

        @pl.when(late)
        def _():
            other_copy(pair, q, dest, part).start()

    def finish_half(unit, r):
        slot = lax.rem(unit, X_SLOTS)
        half_copy(unit, r).wait_recv()
        part = slice(r * hrows, (r + 1) * hrows)
        ysend[unit, part, :] = (own[slot, part, :] + xrecv[slot, part, :]).astype(jnp.bfloat16)
        send_other(unit, pl.ds(r * hrows, hrows))

    def finish(unit):
        pair, kind = split(unit)
        dest, q = task(pair)
        slot = lax.rem(unit, X_SLOTS)
        x_copy(unit).wait_recv()

        @pl.when(kind == 1)
        def _():
            osum[pair] = own[slot] + xrecv[slot]

        joined = (dest == z) & (defers(z - 1, z, q) | defers(z + 1, z, q))

        @pl.when((kind == 0) & joined)
        def _():
            other_copy(pair, q, lax.rem(z + 1, nz), pl.ds(0, rows)).wait_recv()
            ysend[pair] = (own[slot] + xrecv[slot] + orecv[q].astype(jnp.float32)).astype(jnp.bfloat16)

        @pl.when((kind == 0) & jnp.logical_not(joined))
        def _():
            ysend[pair] = (own[slot] + xrecv[slot]).astype(jnp.bfloat16)

        @pl.when(kind == 0)
        def _():
            send_other(pair, pl.ds(0, rows))

    def settle(pair):
        dest, q = task(pair)
        piece = dest * per + q

        @pl.when(jnp.logical_not(defers(z, dest, q)))
        def _():
            y_copy(pair, pl.ds(0, rows)).wait_recv()
            osum[pair] = osum[pair] + yrecv[pair].astype(jnp.float32)

        below = (dest >= z) & (z > 0)
        above = (dest <= z) & (z < nz - 1)

        @pl.when(below)
        def _():
            z_copy(pair, piece, z - 1).wait_recv()
            osum[pair] = osum[pair] + zrecv[piece].astype(jnp.float32)

        @pl.when(above)
        def _():
            place = jnp.where(dest == z, pairs + q, piece)
            z_copy(pair, place, z + 1).wait_recv()
            osum[pair] = osum[pair] + zrecv[place].astype(jnp.float32)

        @pl.when(dest != z)
        def _():
            up = dest > z
            zsend[pair] = osum[pair].astype(jnp.bfloat16)
            place = jnp.where(dest == z - 1, pairs + q, piece)
            z_copy(pair, place, jnp.where(up, z + 1, z - 1)).start()

        @pl.when(dest == z)
        def _():
            g = osum[pair, :, 0:sub]
            u = osum[pair, :, sub:2 * sub]
            at_col = pl.multiple_of(q * sub, 128)
            out_ref[:, pl.ds(at_col, sub)] = (g / (1.0 + jnp.exp(-g)) * u).astype(out_ref.dtype)

    pltpu.make_async_copy(stats.at[1:], stats.at[1:], stat_rsem).wait()
    for r in range(2):
        normalise(r)

        @pl.loop(0, PRE)
        def _(unit):
            if r == 0:
                fetched(unit)
            compute_half(unit, r)

        @pl.loop(0, PRE)
        def _(unit):
            finish_half(unit, r)
            half_copy(unit, r).wait_send()
            if r == 1:
                @pl.when(unit + W_SLOTS < units)
                def _():
                    fetch(unit + W_SLOTS)

    lag = jnp.where(corner, LAG, MID_LAG)

    @pl.loop(PRE, units + 2 * max(LAG, MID_LAG) + 3)
    def _(u):
        @pl.when(u < units)
        def _():
            compute(u)

        @pl.when((u > PRE) & (u <= units))
        def _():
            finish(u - 1)

        j = lax.div(u, 2) - 2 - lag

        @pl.when((lax.rem(u, 2) == 0) & (j >= 0) & (j < pairs))
        def _():
            settle(j)

    for unit in range(units - X_SLOTS, units):
        x_copy(jnp.int32(unit)).wait_send()

    def sent(buf, n, sem):
        pltpu.make_async_copy(buf.at[0:n], buf.at[0:n], sem).wait()

    near = (z == 1) | (z == nz - 2)
    for which, late in ((corner, early), (near, per), (jnp.logical_not(corner | near), 0)):
        @pl.when(which)
        def _():
            sent(ysend, pairs - late, y_ssem)
            if late:
                sent(ysend, late, o_ssem)

    sent(zsend, pairs - per, z_ssem)
    sent(stats, peers - 1, stat_ssem)
    for r in range(2):
        for h in range(2):
            dev, copy = token_copy(h, r)

            @pl.when(dev != me)
            def _():
                copy.wait_send()


def local(tokens, gain, gate_weight, up_weight, gate_mask, up_mask):
    nt = lax.axis_size("tensor")
    ny = 2
    rows, feats = tokens.shape
    depth, ff = gate_weight.shape
    width = ff // nt
    sub = min(SUB, width)
    per = width // sub
    pairs = (nt // ny) * per
    peers = 2 * nt
    dma = pltpu.SemaphoreType.DMA
    hbm = pl.BlockSpec(memory_space=pl.ANY)
    tile = (rows, 2 * sub)
    return pl.pallas_call(
        functools.partial(kernel, nt, ny, sub),
        out_shape=jax.ShapeDtypeStruct((rows, width), jnp.bfloat16),
        in_specs=[hbm] * 6,
        out_specs=pl.BlockSpec(memory_space=pltpu.VMEM),
        scratch_shapes=[
            pltpu.VMEM((rows, feats), jnp.bfloat16),
            pltpu.VMEM((1, gain.shape[0]), jnp.float32),
            pltpu.VMEM((2,) + gate_mask.shape, jnp.int32),
            pltpu.VMEM((peers, 1, rows), jnp.float32),
            pltpu.VMEM((1, rows), jnp.float32),
            pltpu.VMEM((2, rows, depth), jnp.bfloat16),
            pltpu.VMEM((2 * rows, depth), jnp.bfloat16),
            pltpu.VMEM((16, gate_mask.shape[1]), jnp.float32),
            pltpu.VMEM((W_SLOTS, 2, depth, sub), jnp.bfloat16),
            pltpu.VMEM((X_SLOTS,) + tile, jnp.float32),
            pltpu.VMEM((X_SLOTS,) + tile, jnp.float32),
            pltpu.VMEM((X_SLOTS,) + tile, jnp.float32),
            pltpu.VMEM((pairs,) + tile, jnp.float32),
            pltpu.VMEM((pairs,) + tile, jnp.bfloat16),
            pltpu.VMEM((pairs,) + tile, jnp.bfloat16),
            pltpu.VMEM((pairs,) + tile, jnp.bfloat16),
            pltpu.VMEM((pairs + per,) + tile, jnp.bfloat16),
            pltpu.VMEM((per,) + tile, jnp.bfloat16),
            dma((4,)), dma, dma, dma((2, 2)), dma((2, 2)), dma((W_SLOTS,)),
            dma((X_SLOTS,)), dma((X_SLOTS,)), dma((PRE, 2)), dma((PRE, 2)),
            dma, dma((pairs,)), dma, dma((pairs + per,)), dma, dma((per,)),
        ],
        compiler_params=pltpu.CompilerParams(
            collective_id=0, has_side_effects=True, vmem_limit_bytes=44 * 1024 * 1024
        ),
    )(*(pltpu.with_memory_space_constraint(v, pltpu.HBM) for v in (tokens, gain.reshape(1, -1), gate_weight, up_weight, gate_mask, up_mask)))


def solution(mesh):
    in_specs = (
        P(("group", "wide"), "tensor"),
        P("group"),
        P(("group", "wide", "tensor"), None),
        P(("group", "wide", "tensor"), None),
        P("group", None),
        P("group", None),
    )
    out_specs = P(("group", "wide"), "tensor")
    return jax.shard_map(local, mesh=mesh, in_specs=in_specs, out_specs=out_specs, check_vma=False)
```

```python
import functools

import jax
import jax.numpy as jnp
from jax import lax
from jax.experimental import pallas as pl
from jax.experimental.pallas import tpu as pltpu
from jax.sharding import PartitionSpec as P

BS = 64
SUB = 512
LAG = 0
MID_LAG = 7
PRE = 2
LEAD = 6
X_LAG = 1
W_SLOTS = 4
X_SLOTS = 6
EPS = 1e-05
MESH = pl.DeviceIdType.MESH


def kernel(
    nt, ny, sub, tok_hbm, gain_hbm, gw_hbm, uw_hbm, gm_hbm, um_hbm, out_ref,
    tok, gain_all, masks, stats, stat_out, xbuf, xs, mine, spread, wbuf, own, xsend, xrecv, osum,
    ysend, yrecv, zsend, zrecv, orecv,
    in_sem, stat_ssem, stat_rsem, tok_ssem, tok_rsem, wsem, x_ssem, x_rsem, h_ssem, h_rsem,
    y_ssem, y_rsem, z_ssem, z_rsem, o_ssem, o_rsem,
):
    nz = nt // ny
    w = lax.axis_index("wide")
    t = lax.axis_index("tensor")
    z, y = lax.div(t, ny), lax.rem(t, ny)
    me = w * nt + t
    peers = 2 * nt
    rows, feats = tok.shape
    hrows = rows // 2
    depth, ff = gw_hbm.shape
    width = ff // nt
    per = width // sub
    pairs = nz * per
    units = 2 * pairs
    blocks = depth // BS

    def at(dev):
        return {"wide": lax.div(dev, nt), "tensor": lax.rem(dev, nt)}

    barrier = pltpu.get_barrier_semaphore()

    @pl.loop(1, peers)
    def _(d):
        pl.semaphore_signal(
            barrier, inc=1, device_id=at(lax.rem(me + d, peers)), device_id_type=MESH
        )

    loads = (
        pltpu.make_async_copy(tok_hbm, tok, in_sem.at[0]),
        pltpu.make_async_copy(gm_hbm, masks.at[0], in_sem.at[1]),
        pltpu.make_async_copy(um_hbm, masks.at[1], in_sem.at[2]),
        pltpu.make_async_copy(gain_hbm, gain_all, in_sem.at[3]),
    )
    loads[0].start()

    early = max(1, per // 2)
    low = z < nz - 1 - z
    corner = (z == 0) | (z == nz - 1)

    def defers(plane, dest, q):
        to = jnp.where(plane == 1, 0, jnp.where(plane == nz - 2, nz - 1, -1))
        to = jnp.where(plane == 0, 1, jnp.where(plane == nz - 1, nz - 2, to))
        limit = jnp.where((plane == 0) | (plane == nz - 1), early, per)
        return (dest == to) & (q < limit)

    def mid_order(i):
        k = lax.div(i, per)
        right, left = nz - 1 - z, z
        both = jnp.minimum(right, left)
        paired = k < 2 * both
        idx = jnp.where(paired, lax.div(k, 2), k - both)
        is_right = jnp.where(paired, (lax.rem(k, 2) == 0) == (right > left), right > left)
        dest = jnp.where(is_right, nz - 1 - idx, idx)
        dest = jnp.where(k == nz - 1, z, dest)
        return dest, lax.rem(i, per)

    def corner_order(i):
        ahead = jnp.minimum(lax.div(i + 1, 2), early)
        first = (lax.rem(i, 2) == 1) & (i < 2 * early)
        j = i - ahead
        far, near = (nz - 2) * per, (nz - 1) * per - early
        dest = jnp.where(j < far, nz - 1 - lax.div(j, per), jnp.where(j < near, 1, 0))
        q = jnp.where(j < far, lax.rem(j, per), jnp.where(j < near, j - far + early, j - near))
        dest = jnp.where(first, 1, dest)
        q = jnp.where(first, lax.div(i, 2), q)
        return jnp.where(low, dest, nz - 1 - dest), q

    def task(i):
        dest_m, q_m = mid_order(i)
        dest_c, q_c = corner_order(i)
        return jnp.where(corner, dest_c, dest_m), jnp.where(corner, q_c, q_m)

    def split(unit):
        m, odd = lax.div(unit, 2), lax.rem(unit, 2)
        first, last = unit < LEAD, unit >= units - LEAD
        pair = jnp.where(last, pairs - units + unit, m + (LEAD // 2) * (1 - 2 * odd))
        pair = jnp.where(first, unit, pair)
        return pair, jnp.where(first | last, last.astype(jnp.int32), odd)

    def column(unit):
        pair, kind = split(unit)
        y_to = jnp.where(kind == 0, ny - 1 - y, y)
        dest, q = task(pair)
        owner = dest * ny + y_to
        return pl.multiple_of(owner * width + q * sub, 128)

    def weight_copies(unit):
        slot = lax.rem(unit, W_SLOTS)
        cols = pl.ds(column(unit), sub)
        return (
            pltpu.make_async_copy(gw_hbm.at[:, cols], wbuf.at[slot, 0], wsem.at[slot]),
            pltpu.make_async_copy(uw_hbm.at[:, cols], wbuf.at[slot, 1], wsem.at[slot]),
        )

    def fetch(unit):
        for copy in weight_copies(unit):
            copy.start()

    def fetched(unit):
        slot = lax.rem(unit, W_SLOTS)
        pltpu.make_async_copy(wbuf.at[slot], wbuf.at[slot], wsem.at[slot]).wait()

    loads[0].wait()
    total = jnp.zeros((rows, 128), jnp.float32)
    for f in range(0, feats, 128):
        v = tok[:, f:f + 128].astype(jnp.float32)
        total = total + v * v
    line = jnp.sum(total.T, axis=0, keepdims=True)
    stat_out[...] = line
    stats[me] = line

    pl.semaphore_wait(barrier, peers - 1)

    def token_copy(h, r):
        dev = 2 * t + h
        return dev, pltpu.make_async_remote_copy(
            src_ref=tok.at[r * hrows:(r + 1) * hrows, h * depth:(h + 1) * depth],
            dst_ref=xbuf.at[w, r * hrows:(r + 1) * hrows, :],
            send_sem=tok_ssem.at[h, r],
            recv_sem=tok_rsem.at[w, r],
            device_id=at(dev),
            device_id_type=MESH,
        )

    @pl.loop(1, peers)
    def _(d):
        pltpu.make_async_remote_copy(
            src_ref=stat_out, dst_ref=stats.at[me], send_sem=stat_ssem, recv_sem=stat_rsem,
            device_id=at(lax.rem(me + d, peers)), device_id_type=MESH,
        ).start()

    for r in range(2):
        for h in range(2):
            dev, copy = token_copy(h, r)

            @pl.when(dev != me)
            def _():
                copy.start()

            @pl.when(dev == me)
            def _():
                xbuf[w, r * hrows:(r + 1) * hrows, :] = tok[
                    r * hrows:(r + 1) * hrows, h * depth:(h + 1) * depth
                ]

    for copy in loads[1:]:
        copy.start()
    for unit in range(min(W_SLOTS, units)):
        fetch(jnp.int32(unit))

    for copy in loads[1:]:
        copy.wait()
    mrows, mcols = masks.shape[1:]
    pick = (
        lax.broadcasted_iota(jnp.int32, (8, mrows), 1)
        == lax.broadcasted_iota(jnp.int32, (8, mrows), 0) + me * blocks
    ).astype(jnp.float32).astype(jnp.bfloat16)
    for a in range(2):
        kept = masks[a].astype(jnp.float32).astype(jnp.bfloat16)
        mine[a * 8:(a + 1) * 8, :] = jnp.dot(pick, kept, preferred_element_type=jnp.float32)

    gain = gain_all[:, pl.ds(pl.multiple_of(me * depth, 128), depth)]

    def normalise(r):
        for v in range(2):
            @pl.when(v * nt + lax.div(me, 2) != me)
            def _():
                pltpu.make_async_remote_copy(
                    src_ref=tok.at[0:hrows, 0:depth],
                    dst_ref=xbuf.at[v, r * hrows:(r + 1) * hrows, :],
                    send_sem=tok_ssem.at[0, 0], recv_sem=tok_rsem.at[v, r],
                    device_id=at(lax.rem(me + 1, peers)), device_id_type=MESH,
                ).wait_recv()

        for half in range(2):
            v = w if half == 0 else 1 - w
            ssq = jnp.sum(stats[pl.ds(v * nt, nt)], axis=0)
            scale = lax.rsqrt(ssq / (feats * nt) + EPS)
            scale = jnp.broadcast_to(scale, (rows, rows)).T[r * hrows:(r + 1) * hrows, 0:1]
            first = (2 * r + half) * hrows
            xs[first:first + hrows, :] = (
                xbuf[v, r * hrows:(r + 1) * hrows, :].astype(jnp.float32) * scale * gain
            ).astype(jnp.bfloat16)

    everything = pl.ds(0, 2 * sub)

    def half_copy(unit, r, cols=everything):
        slot = lax.rem(unit, X_SLOTS)
        part = pl.ds(r * hrows, hrows)
        return pltpu.make_async_remote_copy(
            src_ref=xsend.at[slot, part, cols], dst_ref=xrecv.at[slot, part, cols],
            send_sem=h_ssem.at[unit, r], recv_sem=h_rsem.at[unit, r],
            device_id={"wide": 1 - w}, device_id_type=MESH,
        )

    def x_copy(unit, cols=everything):
        slot = lax.rem(unit, X_SLOTS)
        return pltpu.make_async_remote_copy(
            src_ref=xsend.at[slot, :, cols], dst_ref=xrecv.at[slot, :, cols],
            send_sem=x_ssem.at[slot], recv_sem=x_rsem.at[slot],
            device_id={"wide": 1 - w}, device_id_type=MESH,
        )

    def y_copy(pair, part):
        return pltpu.make_async_remote_copy(
            src_ref=ysend.at[pair, part, :], dst_ref=yrecv.at[pair, part, :],
            send_sem=y_ssem, recv_sem=y_rsem.at[pair],
            device_id={"tensor": z * ny + (ny - 1 - y)}, device_id_type=MESH,
        )

    def z_copy(pair, place, z_to):
        return pltpu.make_async_remote_copy(
            src_ref=zsend.at[pair], dst_ref=zrecv.at[place],
            send_sem=z_ssem, recv_sem=z_rsem.at[place],
            device_id={"tensor": z_to * ny + y}, device_id_type=MESH,
        )

    def other_copy(pair, q, z_to, part):
        return pltpu.make_async_remote_copy(
            src_ref=ysend.at[pair, part, :], dst_ref=orecv.at[q, part, :],
            send_sem=o_ssem, recv_sem=o_rsem.at[q],
            device_id={"tensor": z_to * ny + y}, device_id_type=MESH,
        )

    def masked(unit):
        slot = lax.rem(unit, W_SLOTS)
        block = lax.div(column(unit), BS)
        here = pltpu.roll(mine[...], lax.rem(mcols - block, mcols), 1)[:, 0:spread.shape[0]]
        mexp = jnp.dot(here.astype(jnp.bfloat16), spread[...], preferred_element_type=jnp.float32)
        for a in range(2):
            kept = []
            for r in range(blocks):
                keep = jnp.broadcast_to(mexp[a * 8 + r:a * 8 + r + 1, :], (BS, sub)).astype(jnp.bfloat16)
                kept.append(wbuf[slot, a, r * BS:(r + 1) * BS, :] * keep)
            yield a, kept

    def mask_ahead(unit):
        slot = lax.rem(unit, W_SLOTS)
        fetched(unit)
        for a, kept in masked(unit):
            for r in range(blocks):
                wbuf[slot, a, r * BS:(r + 1) * BS, :] = kept[r]

    def compute_half(unit, r):
        xslot = lax.rem(unit, X_SLOTS)
        x = xs[2 * r * hrows:2 * (r + 1) * hrows, :]
        for a in range(2):
            part = jnp.dot(x, wbuf[lax.rem(unit, W_SLOTS), a], preferred_element_type=jnp.float32)
            own[xslot, r * hrows:(r + 1) * hrows, a * sub:(a + 1) * sub] = part[:hrows]
            xsend[xslot, r * hrows:(r + 1) * hrows, a * sub:(a + 1) * sub] = part[hrows:]
            half_copy(unit, r, pl.ds(a * sub, sub)).start()

    def compute(unit, ready):
        xslot = lax.rem(unit, X_SLOTS)

        @pl.when(unit >= X_SLOTS + PRE)
        def _():
            x_copy(unit - X_SLOTS).wait_send()

        def keep_part(a, weights):
            part = jnp.dot(xs[...], weights, preferred_element_type=jnp.float32)
            for r in range(2):
                at_row = slice(r * hrows, (r + 1) * hrows)
                own[xslot, at_row, a * sub:(a + 1) * sub] = part[2 * r * hrows:(2 * r + 1) * hrows]
                xsend[xslot, at_row, a * sub:(a + 1) * sub] = part[(2 * r + 1) * hrows:(2 * r + 2) * hrows]
            x_copy(unit, pl.ds(a * sub, sub)).start()

        if ready:
            for a in range(2):
                keep_part(a, wbuf[lax.rem(unit, W_SLOTS), a])
        else:
            fetched(unit)
            for a, kept in masked(unit):
                keep_part(a, jnp.concatenate(kept, axis=0))

        @pl.when(unit + W_SLOTS < units)
        def _():
            fetch(unit + W_SLOTS)

    def send_other(pair, part):
        dest, q = task(pair)
        late = defers(z, dest, q)

        @pl.when(jnp.logical_not(late))
        def _():
            y_copy(pair, part).start()

        @pl.when(late)
        def _():
            other_copy(pair, q, dest, part).start()

    def finish_half(unit, r):
        slot = lax.rem(unit, X_SLOTS)
        half_copy(unit, r).wait_recv()
        part = slice(r * hrows, (r + 1) * hrows)
        ysend[unit, part, :] = (own[slot, part, :] + xrecv[slot, part, :]).astype(jnp.bfloat16)
        send_other(unit, pl.ds(r * hrows, hrows))

    def finish(unit):
        pair, kind = split(unit)
        dest, q = task(pair)
        slot = lax.rem(unit, X_SLOTS)
        x_copy(unit).wait_recv()

        @pl.when(kind == 1)
        def _():
            osum[pair] = own[slot] + xrecv[slot]

        joined = (dest == z) & (defers(z - 1, z, q) | defers(z + 1, z, q))

        @pl.when((kind == 0) & joined)
        def _():
            other_copy(pair, q, lax.rem(z + 1, nz), pl.ds(0, rows)).wait_recv()
            ysend[pair] = (own[slot] + xrecv[slot] + orecv[q].astype(jnp.float32)).astype(jnp.bfloat16)

        @pl.when((kind == 0) & jnp.logical_not(joined))
        def _():
            ysend[pair] = (own[slot] + xrecv[slot]).astype(jnp.bfloat16)

        @pl.when(kind == 0)
        def _():
            send_other(pair, pl.ds(0, rows))

    def settle(pair):
        dest, q = task(pair)
        piece = dest * per + q

        @pl.when(jnp.logical_not(defers(z, dest, q)))
        def _():
            y_copy(pair, pl.ds(0, rows)).wait_recv()
            osum[pair] = osum[pair] + yrecv[pair].astype(jnp.float32)

        below = (dest >= z) & (z > 0)
        above = (dest <= z) & (z < nz - 1)

        @pl.when(below)
        def _():
            z_copy(pair, piece, z - 1).wait_recv()
            osum[pair] = osum[pair] + zrecv[piece].astype(jnp.float32)

        @pl.when(above)
        def _():
            place = jnp.where(dest == z, pairs + q, piece)
            z_copy(pair, place, z + 1).wait_recv()
            osum[pair] = osum[pair] + zrecv[place].astype(jnp.float32)

        @pl.when(dest != z)
        def _():
            up = dest > z
            zsend[pair] = osum[pair].astype(jnp.bfloat16)
            place = jnp.where(dest == z - 1, pairs + q, piece)
            z_copy(pair, place, jnp.where(up, z + 1, z - 1)).start()

        @pl.when(dest == z)
        def _():
            g = osum[pair, :, 0:sub]
            u = osum[pair, :, sub:2 * sub]
            at_col = pl.multiple_of(q * sub, 128)
            out_ref[:, pl.ds(at_col, sub)] = (g / (1.0 + jnp.exp(-g)) * u).astype(out_ref.dtype)

    spread[...] = (
        lax.div(lax.broadcasted_iota(jnp.int32, spread.shape, 1), BS)
        == lax.broadcasted_iota(jnp.int32, spread.shape, 0)
    ).astype(jnp.float32).astype(jnp.bfloat16)

    @pl.loop(0, W_SLOTS)
    def _(unit):
        mask_ahead(unit)

    pltpu.make_async_copy(stats.at[1:], stats.at[1:], stat_rsem).wait()
    for r in range(2):
        normalise(r)

        @pl.loop(0, PRE)
        def _(unit):
            compute_half(unit, r)

        @pl.loop(0, PRE)
        def _(unit):
            finish_half(unit, r)
            half_copy(unit, r).wait_send()
            if r == 1:
                @pl.when(unit + W_SLOTS < units)
                def _():
                    fetch(unit + W_SLOTS)

    lag = jnp.where(corner, LAG, MID_LAG)

    @pl.loop(PRE, units + 2 * max(LAG, MID_LAG) + LEAD + X_LAG)
    def _(u):
        @pl.when(u < W_SLOTS)
        def _():
            compute(u, True)

        @pl.when((u >= W_SLOTS) & (u < units))
        def _():
            compute(u, False)

        @pl.when((u >= PRE + X_LAG) & (u < units + X_LAG))
        def _():
            finish(u - X_LAG)

        j = lax.div(u - LEAD - 1 - X_LAG, 2) - lag

        @pl.when((lax.rem(u - X_LAG, 2) == 1) & (j >= 0) & (j < pairs))
        def _():
            settle(j)

    for unit in range(units - X_SLOTS, units):
        x_copy(jnp.int32(unit)).wait_send()

    def sent(buf, n, sem):
        pltpu.make_async_copy(buf.at[0:n], buf.at[0:n], sem).wait()

    near = (z == 1) | (z == nz - 2)
    for which, late in ((corner, early), (near, per), (jnp.logical_not(corner | near), 0)):
        @pl.when(which)
        def _():
            sent(ysend, pairs - late, y_ssem)
            if late:
                sent(ysend, late, o_ssem)

    sent(zsend, pairs - per, z_ssem)
    sent(stats, peers - 1, stat_ssem)
    for r in range(2):
        for h in range(2):
            dev, copy = token_copy(h, r)

            @pl.when(dev != me)
            def _():
                copy.wait_send()


def local(tokens, gain, gate_weight, up_weight, gate_mask, up_mask):
    nt = lax.axis_size("tensor")
    ny = 2
    rows, feats = tokens.shape
    depth, ff = gate_weight.shape
    width = ff // nt
    sub = min(SUB, width)
    per = width // sub
    pairs = (nt // ny) * per
    peers = 2 * nt
    dma = pltpu.SemaphoreType.DMA
    hbm = pl.BlockSpec(memory_space=pl.ANY)
    tile = (rows, 2 * sub)
    return pl.pallas_call(
        functools.partial(kernel, nt, ny, sub),
        out_shape=jax.ShapeDtypeStruct((rows, width), jnp.bfloat16),
        in_specs=[hbm] * 6,
        out_specs=pl.BlockSpec(memory_space=pltpu.VMEM),
        scratch_shapes=[
            pltpu.VMEM((rows, feats), jnp.bfloat16),
            pltpu.VMEM((1, gain.shape[0]), jnp.float32),
            pltpu.VMEM((2,) + gate_mask.shape, jnp.int32),
            pltpu.VMEM((peers, 1, rows), jnp.float32),
            pltpu.VMEM((1, rows), jnp.float32),
            pltpu.VMEM((2, rows, depth), jnp.bfloat16),
            pltpu.VMEM((2 * rows, depth), jnp.bfloat16),
            pltpu.VMEM((16, gate_mask.shape[1]), jnp.float32),
            pltpu.VMEM((128, sub), jnp.bfloat16),
            pltpu.VMEM((W_SLOTS, 2, depth, sub), jnp.bfloat16),
            pltpu.VMEM((X_SLOTS,) + tile, jnp.float32),
            pltpu.VMEM((X_SLOTS,) + tile, jnp.float32),
            pltpu.VMEM((X_SLOTS,) + tile, jnp.float32),
            pltpu.VMEM((pairs,) + tile, jnp.float32),
            pltpu.VMEM((pairs,) + tile, jnp.bfloat16),
            pltpu.VMEM((pairs,) + tile, jnp.bfloat16),
            pltpu.VMEM((pairs,) + tile, jnp.bfloat16),
            pltpu.VMEM((pairs + per,) + tile, jnp.bfloat16),
            pltpu.VMEM((per,) + tile, jnp.bfloat16),
            dma((4,)), dma, dma, dma((2, 2)), dma((2, 2)), dma((W_SLOTS,)),
            dma((X_SLOTS,)), dma((X_SLOTS,)), dma((PRE, 2)), dma((PRE, 2)),
            dma, dma((pairs,)), dma, dma((pairs + per,)), dma, dma((per,)),
        ],
        compiler_params=pltpu.CompilerParams(
            collective_id=0, has_side_effects=True, vmem_limit_bytes=48 * 1024 * 1024
        ),
    )(*(pltpu.with_memory_space_constraint(v, pltpu.HBM) for v in (tokens, gain.reshape(1, -1), gate_weight, up_weight, gate_mask, up_mask)))


def solution(mesh):
    in_specs = (
        P(("group", "wide"), "tensor"),
        P("group"),
        P(("group", "wide", "tensor"), None),
        P(("group", "wide", "tensor"), None),
        P("group", None),
        P("group", None),
    )
    out_specs = P(("group", "wide"), "tensor")
    return jax.shard_map(local, mesh=mesh, in_specs=in_specs, out_specs=out_specs, check_vma=False)
```

```python
import functools

import jax
import jax.numpy as jnp
from jax import lax
from jax.experimental import pallas as pl
from jax.experimental.pallas import tpu as pltpu
from jax.sharding import PartitionSpec as P

BS = 64
SUB = 512
LAG = 0
MID_LAG = 7
PRE = 2
LEAD = 6
X_LAG = 1
W_SLOTS = 4
X_SLOTS = 6
EPS = 1e-05
MESH = pl.DeviceIdType.MESH


def kernel(
    nt, ny, sub, tok_hbm, gain_hbm, gw_hbm, uw_hbm, gm_hbm, um_hbm, out_ref,
    tok, gain_all, masks, stats, stat_out, xbuf, xs, mine, spread, wbuf, own, xsend, xrecv, osum,
    ysend, yrecv, zsend, zrecv, orecv,
    in_sem, stat_ssem, stat_rsem, tok_ssem, tok_rsem, wsem, x_ssem, x_rsem, h_ssem, h_rsem,
    y_ssem, y_rsem, z_ssem, z_rsem, o_ssem, o_rsem, p_ssem,
):
    nz = nt // ny
    w = lax.axis_index("wide")
    t = lax.axis_index("tensor")
    z, y = lax.div(t, ny), lax.rem(t, ny)
    me = w * nt + t
    peers = 2 * nt
    rows, feats = tok.shape
    hrows = rows // 2
    depth, ff = gw_hbm.shape
    width = ff // nt
    per = width // sub
    pairs = nz * per
    units = 2 * pairs
    blocks = depth // BS

    def at(dev):
        return {"wide": lax.div(dev, nt), "tensor": lax.rem(dev, nt)}

    barrier = pltpu.get_barrier_semaphore()

    @pl.loop(1, peers)
    def _(d):
        pl.semaphore_signal(
            barrier, inc=1, device_id=at(lax.rem(me + d, peers)), device_id_type=MESH
        )

    loads = (
        pltpu.make_async_copy(tok_hbm, tok, in_sem.at[0]),
        pltpu.make_async_copy(gm_hbm, masks.at[0], in_sem.at[1]),
        pltpu.make_async_copy(um_hbm, masks.at[1], in_sem.at[2]),
        pltpu.make_async_copy(gain_hbm, gain_all, in_sem.at[3]),
    )
    loads[0].start()

    early = max(1, per // 2)
    low = z < nz - 1 - z
    corner = (z == 0) | (z == nz - 1)

    def defers(plane, dest, q):
        to = jnp.where(plane == 1, 0, jnp.where(plane == nz - 2, nz - 1, -1))
        to = jnp.where(plane == 0, 1, jnp.where(plane == nz - 1, nz - 2, to))
        limit = jnp.where((plane == 0) | (plane == nz - 1), early, per)
        return (dest == to) & (q < limit)

    kept_rows = rows * 3 // 4
    y_rows, z_rows = pl.ds(0, kept_rows), pl.ds(kept_rows, rows - kept_rows)

    def shares(plane, dest, q):
        to = jnp.where(plane == 0, 1, jnp.where(plane == nz - 1, nz - 2, -1))
        return (dest == to) & (q == early)

    def mid_order(i):
        k = lax.div(i, per)
        right, left = nz - 1 - z, z
        both = jnp.minimum(right, left)
        paired = k < 2 * both
        idx = jnp.where(paired, lax.div(k, 2), k - both)
        is_right = jnp.where(paired, (lax.rem(k, 2) == 0) == (right > left), right > left)
        dest = jnp.where(is_right, nz - 1 - idx, idx)
        dest = jnp.where(k == nz - 1, z, dest)
        return dest, lax.rem(i, per)

    def corner_order(i):
        ahead = jnp.minimum(lax.div(i + 1, 2), early)
        first = (lax.rem(i, 2) == 1) & (i < 2 * early)
        j = i - ahead
        far, near = (nz - 2) * per, (nz - 1) * per - early
        dest = jnp.where(j < far, nz - 1 - lax.div(j, per), jnp.where(j < near, 1, 0))
        q = jnp.where(j < far, lax.rem(j, per), jnp.where(j < near, j - far + early, j - near))
        dest = jnp.where(first, 1, dest)
        q = jnp.where(first, lax.div(i, 2), q)
        return jnp.where(low, dest, nz - 1 - dest), q

    def task(i):
        dest_m, q_m = mid_order(i)
        dest_c, q_c = corner_order(i)
        return jnp.where(corner, dest_c, dest_m), jnp.where(corner, q_c, q_m)

    def split(unit):
        m, odd = lax.div(unit, 2), lax.rem(unit, 2)
        first, last = unit < LEAD, unit >= units - LEAD
        pair = jnp.where(last, pairs - units + unit, m + (LEAD // 2) * (1 - 2 * odd))
        pair = jnp.where(first, unit, pair)
        return pair, jnp.where(first | last, last.astype(jnp.int32), odd)

    def column(unit):
        pair, kind = split(unit)
        y_to = jnp.where(kind == 0, ny - 1 - y, y)
        dest, q = task(pair)
        owner = dest * ny + y_to
        return pl.multiple_of(owner * width + q * sub, 128)

    def weight_copies(unit):
        slot = lax.rem(unit, W_SLOTS)
        cols = pl.ds(column(unit), sub)
        return (
            pltpu.make_async_copy(gw_hbm.at[:, cols], wbuf.at[slot, 0], wsem.at[slot]),
            pltpu.make_async_copy(uw_hbm.at[:, cols], wbuf.at[slot, 1], wsem.at[slot]),
        )

    def fetch(unit):
        for copy in weight_copies(unit):
            copy.start()

    def fetched(unit):
        slot = lax.rem(unit, W_SLOTS)
        pltpu.make_async_copy(wbuf.at[slot], wbuf.at[slot], wsem.at[slot]).wait()

    loads[0].wait()
    total = jnp.zeros((rows, 128), jnp.float32)
    for f in range(0, feats, 128):
        v = tok[:, f:f + 128].astype(jnp.float32)
        total = total + v * v
    line = jnp.sum(total.T, axis=0, keepdims=True)
    stat_out[...] = line
    stats[me] = line

    pl.semaphore_wait(barrier, peers - 1)

    def token_copy(h, r):
        dev = 2 * t + h
        return dev, pltpu.make_async_remote_copy(
            src_ref=tok.at[r * hrows:(r + 1) * hrows, h * depth:(h + 1) * depth],
            dst_ref=xbuf.at[w, r * hrows:(r + 1) * hrows, :],
            send_sem=tok_ssem.at[h, r],
            recv_sem=tok_rsem.at[w, r],
            device_id=at(dev),
            device_id_type=MESH,
        )

    @pl.loop(1, peers)
    def _(d):
        pltpu.make_async_remote_copy(
            src_ref=stat_out, dst_ref=stats.at[me], send_sem=stat_ssem, recv_sem=stat_rsem,
            device_id=at(lax.rem(me + d, peers)), device_id_type=MESH,
        ).start()

    for r in range(2):
        for h in range(2):
            dev, copy = token_copy(h, r)

            @pl.when(dev != me)
            def _():
                copy.start()

            @pl.when(dev == me)
            def _():
                xbuf[w, r * hrows:(r + 1) * hrows, :] = tok[
                    r * hrows:(r + 1) * hrows, h * depth:(h + 1) * depth
                ]

    for copy in loads[1:]:
        copy.start()
    for unit in range(min(W_SLOTS, units)):
        fetch(jnp.int32(unit))

    for copy in loads[1:]:
        copy.wait()
    mrows, mcols = masks.shape[1:]
    pick = (
        lax.broadcasted_iota(jnp.int32, (8, mrows), 1)
        == lax.broadcasted_iota(jnp.int32, (8, mrows), 0) + me * blocks
    ).astype(jnp.float32).astype(jnp.bfloat16)
    for a in range(2):
        kept = masks[a].astype(jnp.float32).astype(jnp.bfloat16)
        mine[a * 8:(a + 1) * 8, :] = jnp.dot(pick, kept, preferred_element_type=jnp.float32)

    gain = gain_all[:, pl.ds(pl.multiple_of(me * depth, 128), depth)]

    def normalise(r):
        for v in range(2):
            @pl.when(v * nt + lax.div(me, 2) != me)
            def _():
                pltpu.make_async_remote_copy(
                    src_ref=tok.at[0:hrows, 0:depth],
                    dst_ref=xbuf.at[v, r * hrows:(r + 1) * hrows, :],
                    send_sem=tok_ssem.at[0, 0], recv_sem=tok_rsem.at[v, r],
                    device_id=at(lax.rem(me + 1, peers)), device_id_type=MESH,
                ).wait_recv()

        for half in range(2):
            v = w if half == 0 else 1 - w
            ssq = jnp.sum(stats[pl.ds(v * nt, nt)], axis=0)
            scale = lax.rsqrt(ssq / (feats * nt) + EPS)
            scale = jnp.broadcast_to(scale, (rows, rows)).T[r * hrows:(r + 1) * hrows, 0:1]
            first = (2 * r + half) * hrows
            xs[first:first + hrows, :] = (
                xbuf[v, r * hrows:(r + 1) * hrows, :].astype(jnp.float32) * scale * gain
            ).astype(jnp.bfloat16)

    everything = pl.ds(0, 2 * sub)

    def half_copy(unit, r, cols=everything):
        slot = lax.rem(unit, X_SLOTS)
        part = pl.ds(r * hrows, hrows)
        return pltpu.make_async_remote_copy(
            src_ref=xsend.at[slot, part, cols], dst_ref=xrecv.at[slot, part, cols],
            send_sem=h_ssem.at[unit, r], recv_sem=h_rsem.at[unit, r],
            device_id={"wide": 1 - w}, device_id_type=MESH,
        )

    def x_copy(unit, cols=everything):
        slot = lax.rem(unit, X_SLOTS)
        return pltpu.make_async_remote_copy(
            src_ref=xsend.at[slot, :, cols], dst_ref=xrecv.at[slot, :, cols],
            send_sem=x_ssem.at[slot], recv_sem=x_rsem.at[slot],
            device_id={"wide": 1 - w}, device_id_type=MESH,
        )

    def y_copy(pair, part, sem=None):
        return pltpu.make_async_remote_copy(
            src_ref=ysend.at[pair, part, :], dst_ref=yrecv.at[pair, part, :],
            send_sem=y_ssem if sem is None else sem, recv_sem=y_rsem.at[pair],
            device_id={"tensor": z * ny + (ny - 1 - y)}, device_id_type=MESH,
        )

    def z_copy(pair, place, z_to):
        return pltpu.make_async_remote_copy(
            src_ref=zsend.at[pair], dst_ref=zrecv.at[place],
            send_sem=z_ssem, recv_sem=z_rsem.at[place],
            device_id={"tensor": z_to * ny + y}, device_id_type=MESH,
        )

    def other_copy(pair, q, z_to, part, sem=None):
        return pltpu.make_async_remote_copy(
            src_ref=ysend.at[pair, part, :], dst_ref=orecv.at[q, part, :],
            send_sem=o_ssem if sem is None else sem, recv_sem=o_rsem.at[q],
            device_id={"tensor": z_to * ny + y}, device_id_type=MESH,
        )

    def masked(unit):
        slot = lax.rem(unit, W_SLOTS)
        block = lax.div(column(unit), BS)
        here = pltpu.roll(mine[...], lax.rem(mcols - block, mcols), 1)[:, 0:spread.shape[0]]
        mexp = jnp.dot(here.astype(jnp.bfloat16), spread[...], preferred_element_type=jnp.float32)
        for a in range(2):
            kept = []
            for r in range(blocks):
                keep = jnp.broadcast_to(mexp[a * 8 + r:a * 8 + r + 1, :], (BS, sub)).astype(jnp.bfloat16)
                kept.append(wbuf[slot, a, r * BS:(r + 1) * BS, :] * keep)
            yield a, kept

    def mask_ahead(unit):
        slot = lax.rem(unit, W_SLOTS)
        fetched(unit)
        for a, kept in masked(unit):
            for r in range(blocks):
                wbuf[slot, a, r * BS:(r + 1) * BS, :] = kept[r]

    def compute_half(unit, r):
        xslot = lax.rem(unit, X_SLOTS)
        x = xs[2 * r * hrows:2 * (r + 1) * hrows, :]
        for a in range(2):
            part = jnp.dot(x, wbuf[lax.rem(unit, W_SLOTS), a], preferred_element_type=jnp.float32)
            own[xslot, r * hrows:(r + 1) * hrows, a * sub:(a + 1) * sub] = part[:hrows]
            xsend[xslot, r * hrows:(r + 1) * hrows, a * sub:(a + 1) * sub] = part[hrows:]
            half_copy(unit, r, pl.ds(a * sub, sub)).start()

    def compute(unit, ready):
        xslot = lax.rem(unit, X_SLOTS)

        @pl.when(unit >= X_SLOTS + PRE)
        def _():
            x_copy(unit - X_SLOTS).wait_send()

        def keep_part(a, weights):
            part = jnp.dot(xs[...], weights, preferred_element_type=jnp.float32)
            for r in range(2):
                at_row = slice(r * hrows, (r + 1) * hrows)
                own[xslot, at_row, a * sub:(a + 1) * sub] = part[2 * r * hrows:(2 * r + 1) * hrows]
                xsend[xslot, at_row, a * sub:(a + 1) * sub] = part[(2 * r + 1) * hrows:(2 * r + 2) * hrows]
            x_copy(unit, pl.ds(a * sub, sub)).start()

        if ready:
            for a in range(2):
                keep_part(a, wbuf[lax.rem(unit, W_SLOTS), a])
        else:
            fetched(unit)
            for a, kept in masked(unit):
                keep_part(a, jnp.concatenate(kept, axis=0))

        @pl.when(unit + W_SLOTS < units)
        def _():
            fetch(unit + W_SLOTS)

    def send_other(pair, part):
        dest, q = task(pair)
        late = defers(z, dest, q)
        shared = shares(z, dest, q)

        @pl.when(jnp.logical_not(late | shared))
        def _():
            y_copy(pair, part).start()

        @pl.when(shared)
        def _():
            y_copy(pair, y_rows, p_ssem.at[0]).start()
            other_copy(pair, q, dest, z_rows, p_ssem.at[1]).start()

        @pl.when(late)
        def _():
            other_copy(pair, q, dest, part).start()

    def finish_half(unit, r):
        slot = lax.rem(unit, X_SLOTS)
        half_copy(unit, r).wait_recv()
        part = slice(r * hrows, (r + 1) * hrows)
        ysend[unit, part, :] = (own[slot, part, :] + xrecv[slot, part, :]).astype(jnp.bfloat16)
        send_other(unit, pl.ds(r * hrows, hrows))

    def finish(unit):
        pair, kind = split(unit)
        dest, q = task(pair)
        slot = lax.rem(unit, X_SLOTS)
        x_copy(unit).wait_recv()

        @pl.when(kind == 1)
        def _():
            osum[pair] = own[slot] + xrecv[slot]

        joined = (dest == z) & (defers(z - 1, z, q) | defers(z + 1, z, q))

        @pl.when((kind == 0) & joined)
        def _():
            other_copy(pair, q, lax.rem(z + 1, nz), pl.ds(0, rows)).wait_recv()
            ysend[pair] = (own[slot] + xrecv[slot] + orecv[q].astype(jnp.float32)).astype(jnp.bfloat16)

        @pl.when((kind == 0) & jnp.logical_not(joined))
        def _():
            ysend[pair] = (own[slot] + xrecv[slot]).astype(jnp.bfloat16)

        @pl.when((kind == 0) & (dest == z) & (shares(z - 1, z, q) | shares(z + 1, z, q)))
        def _():
            other_copy(pair, q, lax.rem(z + 1, nz), z_rows).wait_recv()
            low_rows = slice(kept_rows, rows)
            ysend[pair, low_rows, :] = (
                own[slot, low_rows, :] + xrecv[slot, low_rows, :] + orecv[q, low_rows, :].astype(jnp.float32)
            ).astype(jnp.bfloat16)

        @pl.when(kind == 0)
        def _():
            send_other(pair, pl.ds(0, rows))

    def settle(pair):
        dest, q = task(pair)
        piece = dest * per + q

        shared = shares(z, dest, q)

        @pl.when(jnp.logical_not(defers(z, dest, q) | shared))
        def _():
            y_copy(pair, pl.ds(0, rows)).wait_recv()
            osum[pair] = osum[pair] + yrecv[pair].astype(jnp.float32)

        @pl.when(shared)
        def _():
            y_copy(pair, y_rows).wait_recv()
            top = slice(0, kept_rows)
            osum[pair, top, :] = osum[pair, top, :] + yrecv[pair, top, :].astype(jnp.float32)

        below = (dest >= z) & (z > 0)
        above = (dest <= z) & (z < nz - 1)

        @pl.when(below)
        def _():
            z_copy(pair, piece, z - 1).wait_recv()
            osum[pair] = osum[pair] + zrecv[piece].astype(jnp.float32)

        @pl.when(above)
        def _():
            place = jnp.where(dest == z, pairs + q, piece)
            z_copy(pair, place, z + 1).wait_recv()
            osum[pair] = osum[pair] + zrecv[place].astype(jnp.float32)

        @pl.when(dest != z)
        def _():
            up = dest > z
            zsend[pair] = osum[pair].astype(jnp.bfloat16)
            place = jnp.where(dest == z - 1, pairs + q, piece)
            z_copy(pair, place, jnp.where(up, z + 1, z - 1)).start()

        @pl.when(dest == z)
        def _():
            g = osum[pair, :, 0:sub]
            u = osum[pair, :, sub:2 * sub]
            at_col = pl.multiple_of(q * sub, 128)
            out_ref[:, pl.ds(at_col, sub)] = (g / (1.0 + jnp.exp(-g)) * u).astype(out_ref.dtype)

    spread[...] = (
        lax.div(lax.broadcasted_iota(jnp.int32, spread.shape, 1), BS)
        == lax.broadcasted_iota(jnp.int32, spread.shape, 0)
    ).astype(jnp.float32).astype(jnp.bfloat16)

    @pl.loop(0, W_SLOTS)
    def _(unit):
        mask_ahead(unit)

    pltpu.make_async_copy(stats.at[1:], stats.at[1:], stat_rsem).wait()
    for r in range(2):
        normalise(r)

        @pl.loop(0, PRE)
        def _(unit):
            compute_half(unit, r)

        @pl.loop(0, PRE)
        def _(unit):
            finish_half(unit, r)
            half_copy(unit, r).wait_send()
            if r == 1:
                @pl.when(unit + W_SLOTS < units)
                def _():
                    fetch(unit + W_SLOTS)

    lag = jnp.where(corner, LAG, MID_LAG)

    @pl.loop(PRE, units + 2 * max(LAG, MID_LAG) + LEAD + X_LAG)
    def _(u):
        @pl.when(u < W_SLOTS)
        def _():
            compute(u, True)

        @pl.when((u >= W_SLOTS) & (u < units))
        def _():
            compute(u, False)

        @pl.when((u >= PRE + X_LAG) & (u < units + X_LAG))
        def _():
            finish(u - X_LAG)

        j = lax.div(u - LEAD - 1 - X_LAG, 2) - lag

        @pl.when((lax.rem(u - X_LAG, 2) == 1) & (j >= 0) & (j < pairs))
        def _():
            settle(j)

    for unit in range(units - X_SLOTS, units):
        x_copy(jnp.int32(unit)).wait_send()

    def sent(buf, n, sem):
        pltpu.make_async_copy(buf.at[0:n], buf.at[0:n], sem).wait()

    near = (z == 1) | (z == nz - 2)
    part_way = int(early < per)
    for which, late, some in ((corner, early, part_way), (near, per, 0), (jnp.logical_not(corner | near), 0, 0)):
        @pl.when(which)
        def _():
            sent(ysend, pairs - late - some, y_ssem)
            if some:
                y_copy(0, y_rows, p_ssem.at[0]).wait_send()
                other_copy(0, 0, lax.rem(z + 1, nz), z_rows, p_ssem.at[1]).wait_send()
            if late:
                sent(ysend, late, o_ssem)

    sent(zsend, pairs - per, z_ssem)
    sent(stats, peers - 1, stat_ssem)
    for r in range(2):
        for h in range(2):
            dev, copy = token_copy(h, r)

            @pl.when(dev != me)
            def _():
                copy.wait_send()


def local(tokens, gain, gate_weight, up_weight, gate_mask, up_mask):
    nt = lax.axis_size("tensor")
    ny = 2
    rows, feats = tokens.shape
    depth, ff = gate_weight.shape
    width = ff // nt
    sub = min(SUB, width)
    per = width // sub
    pairs = (nt // ny) * per
    peers = 2 * nt
    dma = pltpu.SemaphoreType.DMA
    hbm = pl.BlockSpec(memory_space=pl.ANY)
    tile = (rows, 2 * sub)
    return pl.pallas_call(
        functools.partial(kernel, nt, ny, sub),
        out_shape=jax.ShapeDtypeStruct((rows, width), jnp.bfloat16),
        in_specs=[hbm] * 6,
        out_specs=pl.BlockSpec(memory_space=pltpu.VMEM),
        scratch_shapes=[
            pltpu.VMEM((rows, feats), jnp.bfloat16),
            pltpu.VMEM((1, gain.shape[0]), jnp.float32),
            pltpu.VMEM((2,) + gate_mask.shape, jnp.int32),
            pltpu.VMEM((peers, 1, rows), jnp.float32),
            pltpu.VMEM((1, rows), jnp.float32),
            pltpu.VMEM((2, rows, depth), jnp.bfloat16),
            pltpu.VMEM((2 * rows, depth), jnp.bfloat16),
            pltpu.VMEM((16, gate_mask.shape[1]), jnp.float32),
            pltpu.VMEM((128, sub), jnp.bfloat16),
            pltpu.VMEM((W_SLOTS, 2, depth, sub), jnp.bfloat16),
            pltpu.VMEM((X_SLOTS,) + tile, jnp.float32),
            pltpu.VMEM((X_SLOTS,) + tile, jnp.float32),
            pltpu.VMEM((X_SLOTS,) + tile, jnp.float32),
            pltpu.VMEM((pairs,) + tile, jnp.float32),
            pltpu.VMEM((pairs,) + tile, jnp.bfloat16),
            pltpu.VMEM((pairs,) + tile, jnp.bfloat16),
            pltpu.VMEM((pairs,) + tile, jnp.bfloat16),
            pltpu.VMEM((pairs + per,) + tile, jnp.bfloat16),
            pltpu.VMEM((per,) + tile, jnp.bfloat16),
            dma((4,)), dma, dma, dma((2, 2)), dma((2, 2)), dma((W_SLOTS,)),
            dma((X_SLOTS,)), dma((X_SLOTS,)), dma((PRE, 2)), dma((PRE, 2)),
            dma, dma((pairs,)), dma, dma((pairs + per,)), dma, dma((per,)), dma((2,)),
        ],
        compiler_params=pltpu.CompilerParams(
            collective_id=0, has_side_effects=True, vmem_limit_bytes=48 * 1024 * 1024
        ),
    )(*(pltpu.with_memory_space_constraint(v, pltpu.HBM) for v in (tokens, gain.reshape(1, -1), gate_weight, up_weight, gate_mask, up_mask)))


def solution(mesh):
    in_specs = (
        P(("group", "wide"), "tensor"),
        P("group"),
        P(("group", "wide", "tensor"), None),
        P(("group", "wide", "tensor"), None),
        P("group", None),
        P("group", None),
    )
    out_specs = P(("group", "wide"), "tensor")
    return jax.shard_map(local, mesh=mesh, in_specs=in_specs, out_specs=out_specs, check_vma=False)
```

```python
import functools

import jax
import jax.numpy as jnp
from jax import lax
from jax.experimental import pallas as pl
from jax.experimental.pallas import tpu as pltpu
from jax.sharding import PartitionSpec as P

BS = 64
SUB = 512
LAG = 0
MID_LAG = 7
PRE = 2
LEAD = 6
X_LAG = 2
W_SLOTS = 4
X_SLOTS = 6
EPS = 1e-05
MESH = pl.DeviceIdType.MESH


def kernel(
    nt, ny, sub, tok_hbm, gain_hbm, gw_hbm, uw_hbm, gm_hbm, um_hbm, out_ref,
    tok, gain_all, masks, stats, stat_out, xbuf, xs, mine, spread, wbuf, own, xsend, xrecv, osum,
    ysend, yrecv, zsend, zrecv, orecv,
    in_sem, stat_ssem, stat_rsem, tok_ssem, tok_rsem, wsem, x_ssem, x_rsem, h_ssem, h_rsem,
    y_ssem, y_rsem, z_ssem, z_rsem, o_ssem, o_rsem, p_ssem,
):
    nz = nt // ny
    w = lax.axis_index("wide")
    t = lax.axis_index("tensor")
    z, y = lax.div(t, ny), lax.rem(t, ny)
    me = w * nt + t
    peers = 2 * nt
    rows, feats = tok.shape
    hrows = rows // 2
    depth, ff = gw_hbm.shape
    width = ff // nt
    per = width // sub
    pairs = nz * per
    units = 2 * pairs
    blocks = depth // BS

    def at(dev):
        return {"wide": lax.div(dev, nt), "tensor": lax.rem(dev, nt)}

    loads = (
        pltpu.make_async_copy(tok_hbm, tok, in_sem.at[0]),
        pltpu.make_async_copy(gm_hbm, masks.at[0], in_sem.at[1]),
        pltpu.make_async_copy(um_hbm, masks.at[1], in_sem.at[2]),
        pltpu.make_async_copy(gain_hbm, gain_all, in_sem.at[3]),
    )
    loads[0].start()

    barrier = pltpu.get_barrier_semaphore()

    @pl.loop(1, peers)
    def _(d):
        pl.semaphore_signal(
            barrier, inc=1, device_id=at(lax.rem(me + d, peers)), device_id_type=MESH
        )

    early = max(1, per // 2)
    low = z < nz - 1 - z
    corner = (z == 0) | (z == nz - 1)

    def defers(plane, dest, q):
        to = jnp.where(plane == 1, 0, jnp.where(plane == nz - 2, nz - 1, -1))
        to = jnp.where(plane == 0, 1, jnp.where(plane == nz - 1, nz - 2, to))
        limit = jnp.where((plane == 0) | (plane == nz - 1), early, per)
        return (dest == to) & (q < limit)

    kept_rows = rows * 3 // 4
    y_rows, z_rows = pl.ds(0, kept_rows), pl.ds(kept_rows, rows - kept_rows)

    def shares(plane, dest, q):
        to = jnp.where(plane == 0, 1, jnp.where(plane == nz - 1, nz - 2, -1))
        return (dest == to) & (q == early)

    def mid_order(i):
        k = lax.div(i, per)
        right, left = nz - 1 - z, z
        both = jnp.minimum(right, left)
        paired = k < 2 * both
        idx = jnp.where(paired, lax.div(k, 2), k - both)
        is_right = jnp.where(paired, (lax.rem(k, 2) == 0) == (right > left), right > left)
        dest = jnp.where(is_right, nz - 1 - idx, idx)
        dest = jnp.where(k == nz - 1, z, dest)
        return dest, lax.rem(i, per)

    def corner_order(i):
        ahead = jnp.minimum(lax.div(i + 1, 2), early)
        first = (lax.rem(i, 2) == 1) & (i < 2 * early)
        j = i - ahead
        far, near = (nz - 2) * per, (nz - 1) * per - early
        dest = jnp.where(j < far, nz - 1 - lax.div(j, per), jnp.where(j < near, 1, 0))
        q = jnp.where(j < far, lax.rem(j, per), jnp.where(j < near, j - far + early, j - near))
        dest = jnp.where(first, 1, dest)
        q = jnp.where(first, lax.div(i, 2), q)
        return jnp.where(low, dest, nz - 1 - dest), q

    def task(i):
        dest_m, q_m = mid_order(i)
        dest_c, q_c = corner_order(i)
        return jnp.where(corner, dest_c, dest_m), jnp.where(corner, q_c, q_m)

    def split(unit):
        m, odd = lax.div(unit, 2), lax.rem(unit, 2)
        first, last = unit < LEAD, unit >= units - LEAD
        pair = jnp.where(last, pairs - units + unit, m + (LEAD // 2) * (1 - 2 * odd))
        pair = jnp.where(first, unit, pair)
        return pair, jnp.where(first | last, last.astype(jnp.int32), odd)

    def column(unit):
        pair, kind = split(unit)
        y_to = jnp.where(kind == 0, ny - 1 - y, y)
        dest, q = task(pair)
        owner = dest * ny + y_to
        return pl.multiple_of(owner * width + q * sub, 128)

    def weight_copies(unit):
        slot = lax.rem(unit, W_SLOTS)
        cols = pl.ds(column(unit), sub)
        return (
            pltpu.make_async_copy(gw_hbm.at[:, cols], wbuf.at[slot, 0], wsem.at[slot]),
            pltpu.make_async_copy(uw_hbm.at[:, cols], wbuf.at[slot, 1], wsem.at[slot]),
        )

    def fetch(unit):
        for copy in weight_copies(unit):
            copy.start()

    def fetched(unit):
        slot = lax.rem(unit, W_SLOTS)
        pltpu.make_async_copy(wbuf.at[slot], wbuf.at[slot], wsem.at[slot]).wait()

    loads[0].wait()
    total = jnp.zeros((rows, 128), jnp.float32)
    for f in range(0, feats, 128):
        v = tok[:, f:f + 128].astype(jnp.float32)
        total = total + v * v
    line = jnp.sum(total.T, axis=0, keepdims=True)
    stat_out[...] = line
    stats[me] = line

    pl.semaphore_wait(barrier, peers - 1)

    def token_copy(h, r):
        dev = 2 * t + h
        return dev, pltpu.make_async_remote_copy(
            src_ref=tok.at[r * hrows:(r + 1) * hrows, h * depth:(h + 1) * depth],
            dst_ref=xbuf.at[w, r * hrows:(r + 1) * hrows, :],
            send_sem=tok_ssem.at[h, r],
            recv_sem=tok_rsem.at[w, r],
            device_id=at(dev),
            device_id_type=MESH,
        )

    @pl.loop(1, peers)
    def _(d):
        pltpu.make_async_remote_copy(
            src_ref=stat_out, dst_ref=stats.at[me], send_sem=stat_ssem, recv_sem=stat_rsem,
            device_id=at(lax.rem(me + d, peers)), device_id_type=MESH,
        ).start()

    for r in range(2):
        for h in range(2):
            dev, copy = token_copy(h, r)

            @pl.when(dev != me)
            def _():
                copy.start()

            @pl.when(dev == me)
            def _():
                xbuf[w, r * hrows:(r + 1) * hrows, :] = tok[
                    r * hrows:(r + 1) * hrows, h * depth:(h + 1) * depth
                ]

    for copy in loads[1:]:
        copy.start()
    for unit in range(min(W_SLOTS, units)):
        fetch(jnp.int32(unit))

    for copy in loads[1:]:
        copy.wait()
    mrows, mcols = masks.shape[1:]
    pick = (
        lax.broadcasted_iota(jnp.int32, (8, mrows), 1)
        == lax.broadcasted_iota(jnp.int32, (8, mrows), 0) + me * blocks
    ).astype(jnp.float32).astype(jnp.bfloat16)
    for a in range(2):
        kept = masks[a].astype(jnp.float32).astype(jnp.bfloat16)
        mine[a * 8:(a + 1) * 8, :] = jnp.dot(pick, kept, preferred_element_type=jnp.float32)

    gain = gain_all[:, pl.ds(pl.multiple_of(me * depth, 128), depth)]

    def normalise(r):
        for v in range(2):
            @pl.when(v * nt + lax.div(me, 2) != me)
            def _():
                pltpu.make_async_remote_copy(
                    src_ref=tok.at[0:hrows, 0:depth],
                    dst_ref=xbuf.at[v, r * hrows:(r + 1) * hrows, :],
                    send_sem=tok_ssem.at[0, 0], recv_sem=tok_rsem.at[v, r],
                    device_id=at(lax.rem(me + 1, peers)), device_id_type=MESH,
                ).wait_recv()

        for half in range(2):
            v = w if half == 0 else 1 - w
            ssq = jnp.sum(stats[pl.ds(v * nt, nt)], axis=0)
            scale = lax.rsqrt(ssq / (feats * nt) + EPS)
            scale = jnp.broadcast_to(scale, (rows, rows)).T[r * hrows:(r + 1) * hrows, 0:1]
            first = (2 * r + half) * hrows
            xs[first:first + hrows, :] = (
                xbuf[v, r * hrows:(r + 1) * hrows, :].astype(jnp.float32) * scale * gain
            ).astype(jnp.bfloat16)

    everything = pl.ds(0, 2 * sub)

    def half_copy(unit, r, cols=everything):
        slot = lax.rem(unit, X_SLOTS)
        part = pl.ds(r * hrows, hrows)
        return pltpu.make_async_remote_copy(
            src_ref=xsend.at[slot, part, cols], dst_ref=xrecv.at[slot, part, cols],
            send_sem=h_ssem.at[unit, r], recv_sem=h_rsem.at[unit, r],
            device_id={"wide": 1 - w}, device_id_type=MESH,
        )

    def x_copy(unit, cols=everything):
        slot = lax.rem(unit, X_SLOTS)
        return pltpu.make_async_remote_copy(
            src_ref=xsend.at[slot, :, cols], dst_ref=xrecv.at[slot, :, cols],
            send_sem=x_ssem.at[slot], recv_sem=x_rsem.at[slot],
            device_id={"wide": 1 - w}, device_id_type=MESH,
        )

    def y_copy(pair, part, sem=None):
        return pltpu.make_async_remote_copy(
            src_ref=ysend.at[pair, part, :], dst_ref=yrecv.at[pair, part, :],
            send_sem=y_ssem if sem is None else sem, recv_sem=y_rsem.at[pair],
            device_id={"tensor": z * ny + (ny - 1 - y)}, device_id_type=MESH,
        )

    def z_copy(pair, place, z_to):
        return pltpu.make_async_remote_copy(
            src_ref=zsend.at[pair], dst_ref=zrecv.at[place],
            send_sem=z_ssem, recv_sem=z_rsem.at[place],
            device_id={"tensor": z_to * ny + y}, device_id_type=MESH,
        )

    def other_copy(pair, q, z_to, part, sem=None):
        return pltpu.make_async_remote_copy(
            src_ref=ysend.at[pair, part, :], dst_ref=orecv.at[q, part, :],
            send_sem=o_ssem if sem is None else sem, recv_sem=o_rsem.at[q],
            device_id={"tensor": z_to * ny + y}, device_id_type=MESH,
        )

    def masked(unit):
        slot = lax.rem(unit, W_SLOTS)
        block = lax.div(column(unit), BS)
        here = pltpu.roll(mine[...], lax.rem(mcols - block, mcols), 1)[:, 0:spread.shape[0]]
        mexp = jnp.dot(here.astype(jnp.bfloat16), spread[...], preferred_element_type=jnp.float32)
        for a in range(2):
            kept = []
            for r in range(blocks):
                keep = jnp.broadcast_to(mexp[a * 8 + r:a * 8 + r + 1, :], (BS, sub)).astype(jnp.bfloat16)
                kept.append(wbuf[slot, a, r * BS:(r + 1) * BS, :] * keep)
            yield a, kept

    def mask_ahead(unit):
        slot = lax.rem(unit, W_SLOTS)
        fetched(unit)
        for a, kept in masked(unit):
            for r in range(blocks):
                wbuf[slot, a, r * BS:(r + 1) * BS, :] = kept[r]

    def compute_half(unit, r):
        xslot = lax.rem(unit, X_SLOTS)
        x = xs[2 * r * hrows:2 * (r + 1) * hrows, :]
        for a in range(2):
            part = jnp.dot(x, wbuf[lax.rem(unit, W_SLOTS), a], preferred_element_type=jnp.float32)
            own[xslot, r * hrows:(r + 1) * hrows, a * sub:(a + 1) * sub] = part[:hrows]
            xsend[xslot, r * hrows:(r + 1) * hrows, a * sub:(a + 1) * sub] = part[hrows:]
            half_copy(unit, r, pl.ds(a * sub, sub)).start()

    def compute(unit, ready):
        xslot = lax.rem(unit, X_SLOTS)

        @pl.when(unit >= X_SLOTS + PRE)
        def _():
            x_copy(unit - X_SLOTS).wait_send()

        def keep_part(a, weights):
            part = jnp.dot(xs[...], weights, preferred_element_type=jnp.float32)
            for r in range(2):
                at_row = slice(r * hrows, (r + 1) * hrows)
                own[xslot, at_row, a * sub:(a + 1) * sub] = part[2 * r * hrows:(2 * r + 1) * hrows]
                xsend[xslot, at_row, a * sub:(a + 1) * sub] = part[(2 * r + 1) * hrows:(2 * r + 2) * hrows]
            x_copy(unit, pl.ds(a * sub, sub)).start()

        if ready:
            for a in range(2):
                keep_part(a, wbuf[lax.rem(unit, W_SLOTS), a])
        else:
            fetched(unit)
            for a, kept in masked(unit):
                keep_part(a, jnp.concatenate(kept, axis=0))

        @pl.when(unit + W_SLOTS < units)
        def _():
            fetch(unit + W_SLOTS)

    def send_other(pair, part):
        dest, q = task(pair)
        late = defers(z, dest, q)
        shared = shares(z, dest, q)

        @pl.when(jnp.logical_not(late | shared))
        def _():
            y_copy(pair, part).start()

        @pl.when(shared)
        def _():
            y_copy(pair, y_rows, p_ssem.at[0]).start()
            other_copy(pair, q, dest, z_rows, p_ssem.at[1]).start()

        @pl.when(late)
        def _():
            other_copy(pair, q, dest, part).start()

    def finish_half(unit, r):
        slot = lax.rem(unit, X_SLOTS)
        half_copy(unit, r).wait_recv()
        part = slice(r * hrows, (r + 1) * hrows)
        ysend[unit, part, :] = (own[slot, part, :] + xrecv[slot, part, :]).astype(jnp.bfloat16)
        send_other(unit, pl.ds(r * hrows, hrows))

    def finish(unit):
        pair, kind = split(unit)
        dest, q = task(pair)
        slot = lax.rem(unit, X_SLOTS)
        x_copy(unit).wait_recv()

        @pl.when(kind == 1)
        def _():
            osum[pair] = own[slot] + xrecv[slot]

        joined = (dest == z) & (defers(z - 1, z, q) | defers(z + 1, z, q))

        @pl.when((kind == 0) & joined)
        def _():
            other_copy(pair, q, lax.rem(z + 1, nz), pl.ds(0, rows)).wait_recv()
            ysend[pair] = (own[slot] + xrecv[slot] + orecv[q].astype(jnp.float32)).astype(jnp.bfloat16)

        @pl.when((kind == 0) & jnp.logical_not(joined))
        def _():
            ysend[pair] = (own[slot] + xrecv[slot]).astype(jnp.bfloat16)

        @pl.when((kind == 0) & (dest == z) & (shares(z - 1, z, q) | shares(z + 1, z, q)))
        def _():
            other_copy(pair, q, lax.rem(z + 1, nz), z_rows).wait_recv()
            low_rows = slice(kept_rows, rows)
            ysend[pair, low_rows, :] = (
                own[slot, low_rows, :] + xrecv[slot, low_rows, :] + orecv[q, low_rows, :].astype(jnp.float32)
            ).astype(jnp.bfloat16)

        @pl.when(kind == 0)
        def _():
            send_other(pair, pl.ds(0, rows))

    def settle(pair):
        dest, q = task(pair)
        piece = dest * per + q

        shared = shares(z, dest, q)

        @pl.when(jnp.logical_not(defers(z, dest, q) | shared))
        def _():
            y_copy(pair, pl.ds(0, rows)).wait_recv()
            osum[pair] = osum[pair] + yrecv[pair].astype(jnp.float32)

        @pl.when(shared)
        def _():
            y_copy(pair, y_rows).wait_recv()
            top = slice(0, kept_rows)
            osum[pair, top, :] = osum[pair, top, :] + yrecv[pair, top, :].astype(jnp.float32)

        below = (dest >= z) & (z > 0)
        above = (dest <= z) & (z < nz - 1)

        @pl.when(below)
        def _():
            z_copy(pair, piece, z - 1).wait_recv()
            osum[pair] = osum[pair] + zrecv[piece].astype(jnp.float32)

        @pl.when(above)
        def _():
            place = jnp.where(dest == z, pairs + q, piece)
            z_copy(pair, place, z + 1).wait_recv()
            osum[pair] = osum[pair] + zrecv[place].astype(jnp.float32)

        @pl.when(dest != z)
        def _():
            up = dest > z
            zsend[pair] = osum[pair].astype(jnp.bfloat16)
            place = jnp.where(dest == z - 1, pairs + q, piece)
            z_copy(pair, place, jnp.where(up, z + 1, z - 1)).start()

        @pl.when(dest == z)
        def _():
            g = osum[pair, :, 0:sub]
            u = osum[pair, :, sub:2 * sub]
            at_col = pl.multiple_of(q * sub, 128)
            out_ref[:, pl.ds(at_col, sub)] = (g / (1.0 + jnp.exp(-g)) * u).astype(out_ref.dtype)

    spread[...] = (
        lax.div(lax.broadcasted_iota(jnp.int32, spread.shape, 1), BS)
        == lax.broadcasted_iota(jnp.int32, spread.shape, 0)
    ).astype(jnp.float32).astype(jnp.bfloat16)

    @pl.loop(0, W_SLOTS)
    def _(unit):
        mask_ahead(unit)

    pltpu.make_async_copy(stats.at[1:], stats.at[1:], stat_rsem).wait()
    for r in range(2):
        normalise(r)

        @pl.loop(0, PRE)
        def _(unit):
            compute_half(unit, r)

        @pl.loop(0, PRE)
        def _(unit):
            finish_half(unit, r)
            half_copy(unit, r).wait_send()
            if r == 1:
                @pl.when(unit + W_SLOTS < units)
                def _():
                    fetch(unit + W_SLOTS)

    lag = jnp.where(corner, LAG, MID_LAG)

    @pl.loop(PRE, units + 2 * max(LAG, MID_LAG) + LEAD + X_LAG)
    def _(u):
        @pl.when(u < W_SLOTS)
        def _():
            compute(u, True)

        @pl.when((u >= W_SLOTS) & (u < units))
        def _():
            compute(u, False)

        @pl.when((u >= PRE + X_LAG) & (u < units + X_LAG))
        def _():
            finish(u - X_LAG)

        j = lax.div(u - LEAD - 1 - X_LAG, 2) - lag

        @pl.when((lax.rem(u - X_LAG, 2) == 1) & (j >= 0) & (j < pairs))
        def _():
            settle(j)

    for unit in range(units - X_SLOTS, units):
        x_copy(jnp.int32(unit)).wait_send()

    def sent(buf, n, sem):
        pltpu.make_async_copy(buf.at[0:n], buf.at[0:n], sem).wait()

    near = (z == 1) | (z == nz - 2)
    part_way = int(early < per)
    for which, late, some in ((corner, early, part_way), (near, per, 0), (jnp.logical_not(corner | near), 0, 0)):
        @pl.when(which)
        def _():
            sent(ysend, pairs - late - some, y_ssem)
            if some:
                y_copy(0, y_rows, p_ssem.at[0]).wait_send()
                other_copy(0, 0, lax.rem(z + 1, nz), z_rows, p_ssem.at[1]).wait_send()
            if late:
                sent(ysend, late, o_ssem)

    sent(zsend, pairs - per, z_ssem)
    sent(stats, peers - 1, stat_ssem)
    for r in range(2):
        for h in range(2):
            dev, copy = token_copy(h, r)

            @pl.when(dev != me)
            def _():
                copy.wait_send()


def local(tokens, gain, gate_weight, up_weight, gate_mask, up_mask):
    nt = lax.axis_size("tensor")
    ny = 2
    rows, feats = tokens.shape
    depth, ff = gate_weight.shape
    width = ff // nt
    sub = min(SUB, width)
    per = width // sub
    pairs = (nt // ny) * per
    peers = 2 * nt
    dma = pltpu.SemaphoreType.DMA
    hbm = pl.BlockSpec(memory_space=pl.ANY)
    tile = (rows, 2 * sub)
    return pl.pallas_call(
        functools.partial(kernel, nt, ny, sub),
        out_shape=jax.ShapeDtypeStruct((rows, width), jnp.bfloat16),
        in_specs=[hbm] * 6,
        out_specs=pl.BlockSpec(memory_space=pltpu.VMEM),
        scratch_shapes=[
            pltpu.VMEM((rows, feats), jnp.bfloat16),
            pltpu.VMEM((1, gain.shape[0]), jnp.float32),
            pltpu.VMEM((2,) + gate_mask.shape, jnp.int32),
            pltpu.VMEM((peers, 1, rows), jnp.float32),
            pltpu.VMEM((1, rows), jnp.float32),
            pltpu.VMEM((2, rows, depth), jnp.bfloat16),
            pltpu.VMEM((2 * rows, depth), jnp.bfloat16),
            pltpu.VMEM((16, gate_mask.shape[1]), jnp.float32),
            pltpu.VMEM((128, sub), jnp.bfloat16),
            pltpu.VMEM((W_SLOTS, 2, depth, sub), jnp.bfloat16),
            pltpu.VMEM((X_SLOTS,) + tile, jnp.float32),
            pltpu.VMEM((X_SLOTS,) + tile, jnp.float32),
            pltpu.VMEM((X_SLOTS,) + tile, jnp.float32),
            pltpu.VMEM((pairs,) + tile, jnp.float32),
            pltpu.VMEM((pairs,) + tile, jnp.bfloat16),
            pltpu.VMEM((pairs,) + tile, jnp.bfloat16),
            pltpu.VMEM((pairs,) + tile, jnp.bfloat16),
            pltpu.VMEM((pairs + per,) + tile, jnp.bfloat16),
            pltpu.VMEM((per,) + tile, jnp.bfloat16),
            dma((4,)), dma, dma, dma((2, 2)), dma((2, 2)), dma((W_SLOTS,)),
            dma((X_SLOTS,)), dma((X_SLOTS,)), dma((PRE, 2)), dma((PRE, 2)),
            dma, dma((pairs,)), dma, dma((pairs + per,)), dma, dma((per,)), dma((2,)),
        ],
        compiler_params=pltpu.CompilerParams(
            collective_id=0, has_side_effects=True, vmem_limit_bytes=48 * 1024 * 1024
        ),
    )(*(pltpu.with_memory_space_constraint(v, pltpu.HBM) for v in (tokens, gain.reshape(1, -1), gate_weight, up_weight, gate_mask, up_mask)))


def solution(mesh):
    in_specs = (
        P(("group", "wide"), "tensor"),
        P("group"),
        P(("group", "wide", "tensor"), None),
        P(("group", "wide", "tensor"), None),
        P("group", None),
        P("group", None),
    )
    out_specs = P(("group", "wide"), "tensor")
    return jax.shard_map(local, mesh=mesh, in_specs=in_specs, out_specs=out_specs, check_vma=False)
```

```python
import functools

import jax
import jax.numpy as jnp
from jax import lax
from jax.experimental import pallas as pl
from jax.experimental.pallas import tpu as pltpu
from jax.sharding import PartitionSpec as P

BS = 64
SUB = 512
LAG = 0
MID_LAG = 6
PRE = 2
LEAD = 6
X_LAG = 2
W_SLOTS = 4
X_SLOTS = 6
EPS = 1e-05
MESH = pl.DeviceIdType.MESH


def kernel(
    nt, ny, sub, tok_hbm, gain_hbm, gw_hbm, uw_hbm, gm_hbm, um_hbm, out_ref,
    tok, gain_all, masks, stats, stat_out, xbuf, xs, mine, spread, wbuf, own, xsend, xrecv, osum,
    ysend, yrecv, zsend, zrecv, orecv,
    in_sem, stat_ssem, stat_rsem, tok_ssem, tok_rsem, wsem, x_ssem, x_rsem, h_ssem, h_rsem,
    y_ssem, y_rsem, z_ssem, z_rsem, o_ssem, o_rsem, p_ssem,
):
    nz = nt // ny
    w = lax.axis_index("wide")
    t = lax.axis_index("tensor")
    z, y = lax.div(t, ny), lax.rem(t, ny)
    me = w * nt + t
    peers = 2 * nt
    rows, feats = tok.shape
    hrows = rows // 2
    depth, ff = gw_hbm.shape
    width = ff // nt
    per = width // sub
    pairs = nz * per
    units = 2 * pairs
    blocks = depth // BS

    def at(dev):
        return {"wide": lax.div(dev, nt), "tensor": lax.rem(dev, nt)}

    loads = (
        pltpu.make_async_copy(tok_hbm, tok, in_sem.at[0]),
        pltpu.make_async_copy(gm_hbm, masks.at[0], in_sem.at[1]),
        pltpu.make_async_copy(um_hbm, masks.at[1], in_sem.at[2]),
        pltpu.make_async_copy(gain_hbm, gain_all, in_sem.at[3]),
    )
    loads[0].start()

    barrier = pltpu.get_barrier_semaphore()

    @pl.loop(1, peers)
    def _(d):
        pl.semaphore_signal(
            barrier, inc=1, device_id=at(lax.rem(me + d, peers)), device_id_type=MESH
        )

    early = max(1, per // 2)
    low = z < nz - 1 - z
    corner = (z == 0) | (z == nz - 1)

    def defers(plane, dest, q):
        to = jnp.where(plane == 1, 0, jnp.where(plane == nz - 2, nz - 1, -1))
        to = jnp.where(plane == 0, 1, jnp.where(plane == nz - 1, nz - 2, to))
        limit = jnp.where((plane == 0) | (plane == nz - 1), early, per)
        return (dest == to) & (q < limit)

    kept_rows = rows * 3 // 4
    y_rows, z_rows = pl.ds(0, kept_rows), pl.ds(kept_rows, rows - kept_rows)

    def shares(plane, dest, q):
        to = jnp.where(plane == 0, 1, jnp.where(plane == nz - 1, nz - 2, -1))
        return (dest == to) & (q == early)

    def mid_order(i):
        k = lax.div(i, per)
        right, left = nz - 1 - z, z
        both = jnp.minimum(right, left)
        paired = k < 2 * both
        idx = jnp.where(paired, lax.div(k, 2), k - both)
        is_right = jnp.where(paired, (lax.rem(k, 2) == 0) == (right > left), right > left)
        dest = jnp.where(is_right, nz - 1 - idx, idx)
        dest = jnp.where(k == nz - 1, z, dest)
        return dest, lax.rem(i, per)

    def corner_order(i):
        ahead = jnp.minimum(lax.div(i + 1, 2), early)
        first = (lax.rem(i, 2) == 1) & (i < 2 * early)
        j = i - ahead
        far, near = (nz - 2) * per, (nz - 1) * per - early
        dest = jnp.where(j < far, nz - 1 - lax.div(j, per), jnp.where(j < near, 1, 0))
        q = jnp.where(j < far, lax.rem(j, per), jnp.where(j < near, j - far + early, j - near))
        dest = jnp.where(first, 1, dest)
        q = jnp.where(first, lax.div(i, 2), q)
        return jnp.where(low, dest, nz - 1 - dest), q

    def task(i):
        dest_m, q_m = mid_order(i)
        dest_c, q_c = corner_order(i)
        return jnp.where(corner, dest_c, dest_m), jnp.where(corner, q_c, q_m)

    def split(unit):
        m, odd = lax.div(unit, 2), lax.rem(unit, 2)
        first, last = unit < LEAD, unit >= units - LEAD
        pair = jnp.where(last, pairs - units + unit, m + (LEAD // 2) * (1 - 2 * odd))
        pair = jnp.where(first, unit, pair)
        return pair, jnp.where(first | last, last.astype(jnp.int32), odd)

    def column(unit):
        pair, kind = split(unit)
        y_to = jnp.where(kind == 0, ny - 1 - y, y)
        dest, q = task(pair)
        owner = dest * ny + y_to
        return pl.multiple_of(owner * width + q * sub, 128)

    def weight_copies(unit):
        slot = lax.rem(unit, W_SLOTS)
        cols = pl.ds(column(unit), sub)
        return (
            pltpu.make_async_copy(gw_hbm.at[:, cols], wbuf.at[slot, 0], wsem.at[slot]),
            pltpu.make_async_copy(uw_hbm.at[:, cols], wbuf.at[slot, 1], wsem.at[slot]),
        )

    def fetch(unit):
        for copy in weight_copies(unit):
            copy.start()

    def fetched(unit):
        slot = lax.rem(unit, W_SLOTS)
        pltpu.make_async_copy(wbuf.at[slot], wbuf.at[slot], wsem.at[slot]).wait()

    loads[0].wait()
    total = jnp.zeros((rows, 128), jnp.float32)
    for f in range(0, feats, 128):
        v = tok[:, f:f + 128].astype(jnp.float32)
        total = total + v * v
    line = jnp.sum(total.T, axis=0, keepdims=True)
    stat_out[...] = line
    stats[me] = line

    pl.semaphore_wait(barrier, peers - 1)

    def token_copy(h, r):
        dev = 2 * t + h
        return dev, pltpu.make_async_remote_copy(
            src_ref=tok.at[r * hrows:(r + 1) * hrows, h * depth:(h + 1) * depth],
            dst_ref=xbuf.at[w, r * hrows:(r + 1) * hrows, :],
            send_sem=tok_ssem.at[h, r],
            recv_sem=tok_rsem.at[w, r],
            device_id=at(dev),
            device_id_type=MESH,
        )

    @pl.loop(1, peers)
    def _(d):
        pltpu.make_async_remote_copy(
            src_ref=stat_out, dst_ref=stats.at[me], send_sem=stat_ssem, recv_sem=stat_rsem,
            device_id=at(lax.rem(me + d, peers)), device_id_type=MESH,
        ).start()

    for r in range(2):
        for h in range(2):
            dev, copy = token_copy(h, r)

            @pl.when(dev != me)
            def _():
                copy.start()

            @pl.when(dev == me)
            def _():
                xbuf[w, r * hrows:(r + 1) * hrows, :] = tok[
                    r * hrows:(r + 1) * hrows, h * depth:(h + 1) * depth
                ]

    for copy in loads[1:]:
        copy.start()
    for unit in range(min(W_SLOTS, units)):
        fetch(jnp.int32(unit))

    for copy in loads[1:]:
        copy.wait()
    mrows, mcols = masks.shape[1:]
    pick = (
        lax.broadcasted_iota(jnp.int32, (8, mrows), 1)
        == lax.broadcasted_iota(jnp.int32, (8, mrows), 0) + me * blocks
    ).astype(jnp.float32).astype(jnp.bfloat16)
    for a in range(2):
        kept = masks[a].astype(jnp.float32).astype(jnp.bfloat16)
        mine[a * 8:(a + 1) * 8, :] = jnp.dot(pick, kept, preferred_element_type=jnp.float32)

    gain = gain_all[:, pl.ds(pl.multiple_of(me * depth, 128), depth)]

    def normalise(r):
        for v in range(2):
            @pl.when(v * nt + lax.div(me, 2) != me)
            def _():
                pltpu.make_async_remote_copy(
                    src_ref=tok.at[0:hrows, 0:depth],
                    dst_ref=xbuf.at[v, r * hrows:(r + 1) * hrows, :],
                    send_sem=tok_ssem.at[0, 0], recv_sem=tok_rsem.at[v, r],
                    device_id=at(lax.rem(me + 1, peers)), device_id_type=MESH,
                ).wait_recv()

        for half in range(2):
            v = w if half == 0 else 1 - w
            ssq = jnp.sum(stats[pl.ds(v * nt, nt)], axis=0)
            scale = lax.rsqrt(ssq / (feats * nt) + EPS)
            scale = jnp.broadcast_to(scale, (rows, rows)).T[r * hrows:(r + 1) * hrows, 0:1]
            first = (2 * r + half) * hrows
            xs[first:first + hrows, :] = (
                xbuf[v, r * hrows:(r + 1) * hrows, :].astype(jnp.float32) * scale * gain
            ).astype(jnp.bfloat16)

    everything = pl.ds(0, 2 * sub)

    def half_copy(unit, r, cols=everything):
        slot = lax.rem(unit, X_SLOTS)
        part = pl.ds(r * hrows, hrows)
        return pltpu.make_async_remote_copy(
            src_ref=xsend.at[slot, part, cols], dst_ref=xrecv.at[slot, part, cols],
            send_sem=h_ssem.at[unit, r], recv_sem=h_rsem.at[unit, r],
            device_id={"wide": 1 - w}, device_id_type=MESH,
        )

    def x_copy(unit, cols=everything):
        slot = lax.rem(unit, X_SLOTS)
        return pltpu.make_async_remote_copy(
            src_ref=xsend.at[slot, :, cols], dst_ref=xrecv.at[slot, :, cols],
            send_sem=x_ssem.at[slot], recv_sem=x_rsem.at[slot],
            device_id={"wide": 1 - w}, device_id_type=MESH,
        )

    def y_copy(pair, part, sem=None):
        return pltpu.make_async_remote_copy(
            src_ref=ysend.at[pair, part, :], dst_ref=yrecv.at[pair, part, :],
            send_sem=y_ssem if sem is None else sem, recv_sem=y_rsem.at[pair],
            device_id={"tensor": z * ny + (ny - 1 - y)}, device_id_type=MESH,
        )

    def z_copy(pair, place, z_to):
        return pltpu.make_async_remote_copy(
            src_ref=zsend.at[pair], dst_ref=zrecv.at[place],
            send_sem=z_ssem, recv_sem=z_rsem.at[place],
            device_id={"tensor": z_to * ny + y}, device_id_type=MESH,
        )

    def other_copy(pair, q, z_to, part, sem=None):
        return pltpu.make_async_remote_copy(
            src_ref=ysend.at[pair, part, :], dst_ref=orecv.at[q, part, :],
            send_sem=o_ssem if sem is None else sem, recv_sem=o_rsem.at[q],
            device_id={"tensor": z_to * ny + y}, device_id_type=MESH,
        )

    def masked(unit):
        slot = lax.rem(unit, W_SLOTS)
        block = lax.div(column(unit), BS)
        here = pltpu.roll(mine[...], lax.rem(mcols - block, mcols), 1)[:, 0:spread.shape[0]]
        mexp = jnp.dot(here.astype(jnp.bfloat16), spread[...], preferred_element_type=jnp.float32)
        for a in range(2):
            kept = []
            for r in range(blocks):
                keep = jnp.broadcast_to(mexp[a * 8 + r:a * 8 + r + 1, :], (BS, sub)).astype(jnp.bfloat16)
                kept.append(wbuf[slot, a, r * BS:(r + 1) * BS, :] * keep)
            yield a, kept

    def mask_ahead(unit):
        slot = lax.rem(unit, W_SLOTS)
        fetched(unit)
        for a, kept in masked(unit):
            for r in range(blocks):
                wbuf[slot, a, r * BS:(r + 1) * BS, :] = kept[r]

    def compute_half(unit, r):
        xslot = lax.rem(unit, X_SLOTS)
        x = xs[2 * r * hrows:2 * (r + 1) * hrows, :]
        for a in range(2):
            part = jnp.dot(x, wbuf[lax.rem(unit, W_SLOTS), a], preferred_element_type=jnp.float32)
            own[xslot, r * hrows:(r + 1) * hrows, a * sub:(a + 1) * sub] = part[:hrows]
            xsend[xslot, r * hrows:(r + 1) * hrows, a * sub:(a + 1) * sub] = part[hrows:]
            half_copy(unit, r, pl.ds(a * sub, sub)).start()

    def compute(unit, ready):
        xslot = lax.rem(unit, X_SLOTS)

        @pl.when(unit >= X_SLOTS + PRE)
        def _():
            x_copy(unit - X_SLOTS).wait_send()

        def keep_part(a, weights):
            part = jnp.dot(xs[...], weights, preferred_element_type=jnp.float32)
            for r in range(2):
                at_row = slice(r * hrows, (r + 1) * hrows)
                own[xslot, at_row, a * sub:(a + 1) * sub] = part[2 * r * hrows:(2 * r + 1) * hrows]
                xsend[xslot, at_row, a * sub:(a + 1) * sub] = part[(2 * r + 1) * hrows:(2 * r + 2) * hrows]
            x_copy(unit, pl.ds(a * sub, sub)).start()

        if ready:
            for a in range(2):
                keep_part(a, wbuf[lax.rem(unit, W_SLOTS), a])
        else:
            fetched(unit)
            for a, kept in masked(unit):
                keep_part(a, jnp.concatenate(kept, axis=0))

        @pl.when(unit + W_SLOTS < units)
        def _():
            fetch(unit + W_SLOTS)

    def send_other(pair, part):
        dest, q = task(pair)
        late = defers(z, dest, q)
        shared = shares(z, dest, q)

        @pl.when(jnp.logical_not(late | shared))
        def _():
            y_copy(pair, part).start()

        @pl.when(shared)
        def _():
            y_copy(pair, y_rows, p_ssem.at[0]).start()
            other_copy(pair, q, dest, z_rows, p_ssem.at[1]).start()

        @pl.when(late)
        def _():
            other_copy(pair, q, dest, part).start()

    def finish_half(unit, r):
        slot = lax.rem(unit, X_SLOTS)
        half_copy(unit, r).wait_recv()
        part = slice(r * hrows, (r + 1) * hrows)
        ysend[unit, part, :] = (own[slot, part, :] + xrecv[slot, part, :]).astype(jnp.bfloat16)
        send_other(unit, pl.ds(r * hrows, hrows))

    def finish(unit):
        pair, kind = split(unit)
        dest, q = task(pair)
        slot = lax.rem(unit, X_SLOTS)
        x_copy(unit).wait_recv()

        @pl.when(kind == 1)
        def _():
            osum[pair] = own[slot] + xrecv[slot]

        joined = (dest == z) & (defers(z - 1, z, q) | defers(z + 1, z, q))

        @pl.when((kind == 0) & joined)
        def _():
            other_copy(pair, q, lax.rem(z + 1, nz), pl.ds(0, rows)).wait_recv()
            ysend[pair] = (own[slot] + xrecv[slot] + orecv[q].astype(jnp.float32)).astype(jnp.bfloat16)

        @pl.when((kind == 0) & jnp.logical_not(joined))
        def _():
            ysend[pair] = (own[slot] + xrecv[slot]).astype(jnp.bfloat16)

        @pl.when((kind == 0) & (dest == z) & (shares(z - 1, z, q) | shares(z + 1, z, q)))
        def _():
            other_copy(pair, q, lax.rem(z + 1, nz), z_rows).wait_recv()
            low_rows = slice(kept_rows, rows)
            ysend[pair, low_rows, :] = (
                own[slot, low_rows, :] + xrecv[slot, low_rows, :] + orecv[q, low_rows, :].astype(jnp.float32)
            ).astype(jnp.bfloat16)

        @pl.when(kind == 0)
        def _():
            send_other(pair, pl.ds(0, rows))

    def settle(pair):
        dest, q = task(pair)
        piece = dest * per + q

        shared = shares(z, dest, q)

        @pl.when(jnp.logical_not(defers(z, dest, q) | shared))
        def _():
            y_copy(pair, pl.ds(0, rows)).wait_recv()
            osum[pair] = osum[pair] + yrecv[pair].astype(jnp.float32)

        @pl.when(shared)
        def _():
            y_copy(pair, y_rows).wait_recv()
            top = slice(0, kept_rows)
            osum[pair, top, :] = osum[pair, top, :] + yrecv[pair, top, :].astype(jnp.float32)

        below = (dest >= z) & (z > 0)
        above = (dest <= z) & (z < nz - 1)

        @pl.when(below)
        def _():
            z_copy(pair, piece, z - 1).wait_recv()
            osum[pair] = osum[pair] + zrecv[piece].astype(jnp.float32)

        @pl.when(above)
        def _():
            place = jnp.where(dest == z, pairs + q, piece)
            z_copy(pair, place, z + 1).wait_recv()
            osum[pair] = osum[pair] + zrecv[place].astype(jnp.float32)

        @pl.when(dest != z)
        def _():
            up = dest > z
            zsend[pair] = osum[pair].astype(jnp.bfloat16)
            place = jnp.where(dest == z - 1, pairs + q, piece)
            z_copy(pair, place, jnp.where(up, z + 1, z - 1)).start()

        @pl.when(dest == z)
        def _():
            g = osum[pair, :, 0:sub]
            u = osum[pair, :, sub:2 * sub]
            at_col = pl.multiple_of(q * sub, 128)
            out_ref[:, pl.ds(at_col, sub)] = (g / (1.0 + jnp.exp(-g)) * u).astype(out_ref.dtype)

    spread[...] = (
        lax.div(lax.broadcasted_iota(jnp.int32, spread.shape, 1), BS)
        == lax.broadcasted_iota(jnp.int32, spread.shape, 0)
    ).astype(jnp.float32).astype(jnp.bfloat16)

    @pl.loop(0, W_SLOTS)
    def _(unit):
        mask_ahead(unit)

    pltpu.make_async_copy(stats.at[1:], stats.at[1:], stat_rsem).wait()
    for r in range(2):
        normalise(r)

        @pl.loop(0, PRE)
        def _(unit):
            compute_half(unit, r)

        @pl.loop(0, PRE)
        def _(unit):
            finish_half(unit, r)
            half_copy(unit, r).wait_send()
            if r == 1:
                @pl.when(unit + W_SLOTS < units)
                def _():
                    fetch(unit + W_SLOTS)

    lag = jnp.where(corner, LAG, MID_LAG)

    @pl.loop(PRE, units + 2 * max(LAG, MID_LAG) + LEAD + X_LAG)
    def _(u):
        @pl.when(u < W_SLOTS)
        def _():
            compute(u, True)

        @pl.when((u >= W_SLOTS) & (u < units))
        def _():
            compute(u, False)

        @pl.when((u >= PRE + X_LAG) & (u < units + X_LAG))
        def _():
            finish(u - X_LAG)

        j = lax.div(u - LEAD - 1 - X_LAG, 2) - lag

        @pl.when((lax.rem(u - X_LAG, 2) == 1) & (j >= 0) & (j < pairs))
        def _():
            settle(j)

    for unit in range(units - X_SLOTS, units):
        x_copy(jnp.int32(unit)).wait_send()

    def sent(buf, n, sem):
        pltpu.make_async_copy(buf.at[0:n], buf.at[0:n], sem).wait()

    near = (z == 1) | (z == nz - 2)
    part_way = int(early < per)
    for which, late, some in ((corner, early, part_way), (near, per, 0), (jnp.logical_not(corner | near), 0, 0)):
        @pl.when(which)
        def _():
            sent(ysend, pairs - late - some, y_ssem)
            if some:
                y_copy(0, y_rows, p_ssem.at[0]).wait_send()
                other_copy(0, 0, lax.rem(z + 1, nz), z_rows, p_ssem.at[1]).wait_send()
            if late:
                sent(ysend, late, o_ssem)

    sent(zsend, pairs - per, z_ssem)
    sent(stats, peers - 1, stat_ssem)
    for r in range(2):
        for h in range(2):
            dev, copy = token_copy(h, r)

            @pl.when(dev != me)
            def _():
                copy.wait_send()


def local(tokens, gain, gate_weight, up_weight, gate_mask, up_mask):
    nt = lax.axis_size("tensor")
    ny = 2
    rows, feats = tokens.shape
    depth, ff = gate_weight.shape
    width = ff // nt
    sub = min(SUB, width)
    per = width // sub
    pairs = (nt // ny) * per
    peers = 2 * nt
    dma = pltpu.SemaphoreType.DMA
    hbm = pl.BlockSpec(memory_space=pl.ANY)
    tile = (rows, 2 * sub)
    return pl.pallas_call(
        functools.partial(kernel, nt, ny, sub),
        out_shape=jax.ShapeDtypeStruct((rows, width), jnp.bfloat16),
        in_specs=[hbm] * 6,
        out_specs=pl.BlockSpec(memory_space=pltpu.VMEM),
        scratch_shapes=[
            pltpu.VMEM((rows, feats), jnp.bfloat16),
            pltpu.VMEM((1, gain.shape[0]), jnp.float32),
            pltpu.VMEM((2,) + gate_mask.shape, jnp.int32),
            pltpu.VMEM((peers, 1, rows), jnp.float32),
            pltpu.VMEM((1, rows), jnp.float32),
            pltpu.VMEM((2, rows, depth), jnp.bfloat16),
            pltpu.VMEM((2 * rows, depth), jnp.bfloat16),
            pltpu.VMEM((16, gate_mask.shape[1]), jnp.float32),
            pltpu.VMEM((128, sub), jnp.bfloat16),
            pltpu.VMEM((W_SLOTS, 2, depth, sub), jnp.bfloat16),
            pltpu.VMEM((X_SLOTS,) + tile, jnp.float32),
            pltpu.VMEM((X_SLOTS,) + tile, jnp.float32),
            pltpu.VMEM((X_SLOTS,) + tile, jnp.float32),
            pltpu.VMEM((pairs,) + tile, jnp.float32),
            pltpu.VMEM((pairs,) + tile, jnp.bfloat16),
            pltpu.VMEM((pairs,) + tile, jnp.bfloat16),
            pltpu.VMEM((pairs,) + tile, jnp.bfloat16),
            pltpu.VMEM((pairs + per,) + tile, jnp.bfloat16),
            pltpu.VMEM((per,) + tile, jnp.bfloat16),
            dma((4,)), dma, dma, dma((2, 2)), dma((2, 2)), dma((W_SLOTS,)),
            dma((X_SLOTS,)), dma((X_SLOTS,)), dma((PRE, 2)), dma((PRE, 2)),
            dma, dma((pairs,)), dma, dma((pairs + per,)), dma, dma((per,)), dma((2,)),
        ],
        compiler_params=pltpu.CompilerParams(
            collective_id=0, has_side_effects=True, vmem_limit_bytes=48 * 1024 * 1024
        ),
    )(*(pltpu.with_memory_space_constraint(v, pltpu.HBM) for v in (tokens, gain.reshape(1, -1), gate_weight, up_weight, gate_mask, up_mask)))


def solution(mesh):
    in_specs = (
        P(("group", "wide"), "tensor"),
        P("group"),
        P(("group", "wide", "tensor"), None),
        P(("group", "wide", "tensor"), None),
        P("group", None),
        P("group", None),
    )
    out_specs = P(("group", "wide"), "tensor")
    return jax.shard_map(local, mesh=mesh, in_specs=in_specs, out_specs=out_specs, check_vma=False)
```
